768 devices in a mesh: gx: 12 (over z), gy: 64 (over x, y, core).
Axes of the slice: x: 4, y: 8, z: 12, core: 2. Of those that a mesh axis runs over, the one named last changes fastest.
Arguments:
- flow_state: float32 [4, 96, 512, 128], P(None, 'gx', 'gy'), may hold values from -4.5 to 4.5, as said below
- building_height: int32 [12, 64], P('gx', 'gy'), may hold values from 0 to 8
- pressure_old: float32 [96, 512, 128], P('gx', 'gy'), may hold values from -0.3 to 0.3
Outputs:
- new_state: float32 [4, 96, 512, 128], P(None, 'gx', 'gy')
- pressure: float32 [96, 512, 128], P('gx', 'gy')
The draws below stay inside these ranges and needn't reach their ends.
Inputs may be any that keep to these rules, and one draw needn't show every extreme that they name: `flow_state`: velocity and temperature fluctuations whose size varies across the district.
All inputs are finite; a program needn't handle non-finite values.
Results may differ from the reference program's by a relative error of at most 0.0003.
Values sent between devices are 32-bit elements; how exact they have to be, the bound alone decides.
No kernel may reach another device: no remote copies, remote signals or barrier semaphores. Data moves between devices by JAX's collectives and lax.ppermute only.
A program may use at most 32 MiB of HBM per device.

```python
import math
import jax
import jax.numpy as jnp
import numpy as np
from jax import lax

EZ = 16
ITERS = 2
NEX = 12
NEY = 64
NX = 96
NY = 512
NZ = 128


def draw_flow_state(key, part):
    across = (jnp.arange(NX, dtype=jnp.float32) + 0.5) / NX
    along = (jnp.arange(NY, dtype=jnp.float32) + 0.5) / NY
    ramp = (1.0 + 2.0 * across)[:, None] * (1.0 + 2.0 * along)[None, :] / 6.0
    ramp = ramp[None, :, :, None]
    values = jax.random.normal(key, (4, NX, NY, NZ), jnp.float32) * ramp
    return jnp.clip(values, -4.5, 4.5)


def plant(entries, stream_key, least, largest):
    longest = entries.shape.index(max(entries.shape))
    spots = []
    for shift in (0, 1):
        where = [jax.random.randint(jax.random.fold_in(stream_key, axis), (), 0, length) for axis, length in enumerate(entries.shape)]
        where[longest] = (where[longest] + shift) % entries.shape[longest]
        spots.append(tuple(where))
    return entries.at[spots[0]].set(least).at[spots[1]].set(largest)


def steps_of(stream_key, dims, shards, low, largest):
    loudness, own = 1.0, jax.random.fold_in(stream_key, 6)
    for dim, blocks in shards:
        draws = jnp.exp(jax.random.uniform(jax.random.fold_in(own, dim), (blocks,), jnp.float32, low / len(shards), largest / len(shards)))
        loudness = loudness * jnp.repeat(draws, dims[dim] // blocks).reshape([-1 if axis == dim else 1 for axis in range(len(dims))])
    return loudness


def normal_values(stream_key, dims, spread, most, shards=(), kind=jnp.bfloat16):
    drawn = spread * jax.random.normal(stream_key, dims, jnp.float32)
    if shards:
        drawn = drawn * steps_of(stream_key, dims, shards, -0.22, 0.18)
    return jnp.clip(drawn, -most, most).astype(kind)


def setup_inputs(seed: int = 0) -> dict:
    arg_keys = jax.random.split(jax.random.key(seed), 4)
    return {
        "flow_state": draw_flow_state(jax.random.fold_in(arg_keys[3], 71), 0),
        "building_height": plant(jax.random.randint(arg_keys[1], (NEX, NEY), 0, EZ // 2 + 1), jax.random.fold_in(arg_keys[1], 1), 0, (EZ // 2 + 1) - 1).astype(jnp.int32),
        "pressure_old": normal_values(arg_keys[2], (NX, NY, NZ), 0.05, 0.3, ((0, 12), (1, 64)), jnp.float32),
    }


HIGHEST = lax.Precision.HIGHEST
viscosity = 0.05
time_step = 0.01
drag_strength = 20.0
heating = 40.0
buoyancy = 10.0
helmholtz_shift = 0.001
local_shift = 0.5
coarse_shift = 0.02
gll_points = (-1.0, -0.8717401485096066, -0.5917001814331423, -0.2092992179024789, 0.2092992179024789, 0.5917001814331423, 0.8717401485096066, 1.0)

def legendre_seven(points):
    squared = points * points
    return points * (((429.0 * squared - 693.0) * squared + 315.0) * squared - 35.0) / 16.0

def jacobi_eigen(matrix):
    current = np.array(matrix)
    basis = np.eye(8)
    for rounds in range(12):
        for first in range(7):
            for second in range(first + 1, 8):
                rotation_angle = 0.5 * math.atan2(2.0 * float(current[first, second]), float(current[second, second] - current[first, first]))
                cosine = math.cos(rotation_angle)
                sine = math.sin(rotation_angle)
                rotation = np.eye(8)
                rotation[first, first] = cosine
                rotation[second, second] = cosine
                rotation[first, second] = sine
                rotation[second, first] = -sine
                current = rotation.T @ current @ rotation
                basis = basis @ rotation
    return (np.sum(current * np.eye(8), axis=0), basis)

def gll_tables():
    gll_nodes = np.array(gll_points)
    values = legendre_seven(gll_nodes)
    weights = 2.0 / (56.0 * values * values)
    differ = gll_nodes[:, None] - gll_nodes[None, :] + np.eye(8)
    derivative = values[:, None] / values[None, :] / differ * (1.0 - np.eye(8))
    derivative = derivative + np.eye(8) * np.array([-14.0, 0.0, 0.0, 0.0, 0.0, 0.0, 0.0, 14.0])[None, :]
    stiffness = derivative.T @ (weights[:, None] * derivative)
    scaled = stiffness / np.sqrt(np.outer(weights, weights))
    scaled = 0.5 * (scaled + scaled.T)
    eigen_values, eigen_vectors = jacobi_eigen(scaled)
    eigen_basis = eigen_vectors / np.sqrt(weights)[:, None]
    return (gll_nodes, weights, derivative, eigen_basis, np.maximum(eigen_values, 0.0))

def tables():
    return tuple((jnp.asarray(table, dtype=jnp.float32) for table in gll_tables()))

def along_x(field, matrix):
    first, second, third, fourth = field.shape
    blocks = field.reshape(first, second // 8, 8, third, fourth)
    return jnp.einsum('ij,cejyz->ceiyz', matrix, blocks, precision=HIGHEST).reshape(field.shape)

def along_y(field, matrix):
    first, second, third, fourth = field.shape
    blocks = field.reshape(first, second, third // 8, 8, fourth)
    return jnp.einsum('ij,cxejz->cxeiz', matrix, blocks, precision=HIGHEST).reshape(field.shape)

def along_z(field, matrix):
    first, second, third, fourth = field.shape
    blocks = field.reshape(first, second, third, fourth // 8, 8)
    return jnp.einsum('ij,cxyej->cxyei', matrix, blocks, precision=HIGHEST).reshape(field.shape)

def weight_grid(weights, width, depth, height):
    return jnp.tile(weights, width // 8)[:, None, None] * jnp.tile(weights, depth // 8)[None, :, None] * jnp.tile(weights, height // 8)[None, None, :]

def face_counts(count):
    index = jnp.arange(count, dtype=jnp.int32) % 8
    return jnp.where((index == 0) | (index == 7), 2.0, 1.0).astype(jnp.float32)

def multiplicity(width, depth, height):
    vertical_index = jnp.arange(height, dtype=jnp.int32)
    ends = (vertical_index == 0) | (vertical_index == height - 1)
    vertical = jnp.where(ends, 1.0, face_counts(height)).astype(jnp.float32)
    return face_counts(width)[:, None, None] * face_counts(depth)[None, :, None] * vertical[None, None, :]

def canopy_mask(building_height, height):
    column = jnp.repeat(jnp.repeat(building_height, 8, axis=0), 8, axis=1)
    layer = jnp.arange(height, dtype=jnp.int32) // 8
    return (layer[None, None, :] < column[:, :, None]).astype(jnp.float32)

def stiffness_action(field, mass, derivative):
    term = along_x(mass * along_x(field, derivative), derivative.T)
    term = term + along_y(mass * along_y(field, derivative), derivative.T)
    return term + along_z(mass * along_z(field, derivative), derivative.T)

def pair_z(field):
    first, second, third, fourth = field.shape
    blocks = field.reshape(first, second, third, fourth // 8, 8)
    sums = blocks[..., :-1, 7] + blocks[..., 1:, 0]
    starts = jnp.concatenate([blocks[..., :1, 0], sums], axis=3)
    finals = jnp.concatenate([sums, blocks[..., -1:, 7]], axis=3)
    return jnp.concatenate([starts[..., None], blocks[..., 1:7], finals[..., None]], axis=4).reshape(field.shape)

def pair_x(field):
    first, second, third, fourth = field.shape
    blocks = field.reshape(first, second // 8, 8, third, fourth)
    sums = blocks[:, :, 7] + jnp.roll(blocks[:, :, 0], -1, axis=1)
    return jnp.concatenate([jnp.roll(sums, 1, axis=1)[:, :, None], blocks[:, :, 1:7], sums[:, :, None]], axis=2).reshape(field.shape)

def pair_y(field):
    first, second, third, fourth = field.shape
    blocks = field.reshape(first, second, third // 8, 8, fourth)
    sums = blocks[:, :, :, 7] + jnp.roll(blocks[:, :, :, 0], -1, axis=2)
    return jnp.concatenate([jnp.roll(sums, 1, axis=2)[:, :, :, None], blocks[:, :, :, 1:7], sums[:, :, :, None]], axis=3).reshape(field.shape)

def assemble_global(field):
    return pair_z(pair_y(pair_x(field)))

def local_solve(field, eigen_basis, eigen_values):
    first, width, depth, height = field.shape
    spectrum = jnp.tile(eigen_values, width // 8)[:, None, None] + jnp.tile(eigen_values, depth // 8)[None, :, None] + jnp.tile(eigen_values, height // 8)[None, None, :]
    inverse = eigen_basis.T
    modal = along_z(along_y(along_x(field, inverse), inverse), inverse)
    modal = modal / (spectrum + local_shift)
    return along_z(along_y(along_x(modal, eigen_basis), eigen_basis), eigen_basis)

def interpolation(width, periodic, gll_nodes):
    count = width // 8
    columns = count if periodic else count + 1
    position = jnp.tile(gll_nodes, count)
    element = jnp.arange(width, dtype=jnp.int32) // 8
    following = (element + 1) % columns if periodic else element + 1
    target = jnp.arange(columns, dtype=jnp.int32)[None, :]
    left = jnp.where(target == element[:, None], (1.0 - position)[:, None] / 2.0, 0.0)
    right = jnp.where(target == following[:, None], (1.0 + position)[:, None] / 2.0, 0.0)
    return (left + right).astype(jnp.float32)

def restrict(field, across, along, vertical):
    reduced = jnp.einsum('xa,xyz->ayz', across, field, precision=HIGHEST)
    reduced = jnp.einsum('yb,ayz->abz', along, reduced, precision=HIGHEST)
    return jnp.einsum('zc,abz->abc', vertical, reduced, precision=HIGHEST)

def prolong(coarse, across, along, vertical):
    fine = jnp.einsum('zc,abc->abz', vertical, coarse, precision=HIGHEST)
    fine = jnp.einsum('yb,abz->ayz', along, fine, precision=HIGHEST)
    return jnp.einsum('xa,ayz->xyz', across, fine, precision=HIGHEST)

def spectral_tables(count):
    index = jnp.arange(count, dtype=jnp.int32)
    angle = 2.0 * np.pi / count * (index[:, None] * index[None, :] % count).astype(jnp.float32)
    hartley = (jnp.cos(angle) + jnp.sin(angle)) / np.sqrt(count)
    eigen = 2.0 - 2.0 * jnp.cos(2.0 * np.pi / count * index.astype(jnp.float32))
    return (hartley.astype(jnp.float32), eigen.astype(jnp.float32))

def cosine_tables(count):
    index = jnp.arange(count, dtype=jnp.int32).astype(jnp.float32)
    angle = np.pi / count * (index[:, None] + 0.5) * index[None, :]
    norms = jnp.where(index == 0, np.sqrt(1.0 / count), np.sqrt(2.0 / count))
    basis = jnp.cos(angle) * norms[None, :]
    eigen = 2.0 - 2.0 * jnp.cos(np.pi / count * index)
    return (basis.astype(jnp.float32), eigen.astype(jnp.float32))

def coarse_solve(grid):
    first, second, third = grid.shape
    hartley_x, eigen_x = spectral_tables(first)
    hartley_y, eigen_y = spectral_tables(second)
    cosine_z, eigen_z = cosine_tables(third)
    modes = jnp.einsum('ai,ijk->ajk', hartley_x, grid, precision=HIGHEST)
    modes = jnp.einsum('bj,ajk->abk', hartley_y, modes, precision=HIGHEST)
    modes = jnp.einsum('kc,abk->abc', cosine_z, modes, precision=HIGHEST)
    modes = modes / (2.0 * (eigen_x[:, None, None] + eigen_y[None, :, None] + eigen_z[None, None, :]) + coarse_shift)
    values = jnp.einsum('kc,abc->abk', cosine_z, modes, precision=HIGHEST)
    values = jnp.einsum('bj,ajk->abk', hartley_y, values, precision=HIGHEST)
    return jnp.einsum('ai,ijk->ajk', hartley_x, values, precision=HIGHEST)

def provisional_state(flow_state, mass, counts, canopy, derivative, assemble):
    speed = jnp.sqrt(flow_state[0] * flow_state[0] + flow_state[1] * flow_state[1] + flow_state[2] * flow_state[2])
    drag = drag_strength * canopy * speed
    forcing = jnp.stack([-drag * flow_state[0], -drag * flow_state[1], -drag * flow_state[2] + buoyancy * flow_state[3], heating * canopy])
    advection = -(flow_state[0] * along_x(flow_state, derivative) + flow_state[1] * along_y(flow_state, derivative) + flow_state[2] * along_z(flow_state, derivative))
    rate = mass * (advection + forcing) - viscosity * stiffness_action(flow_state, mass, derivative)
    updated = flow_state + time_step * assemble(rate) / (mass * counts)
    height = flow_state.shape[3]
    vertical_index = jnp.arange(height, dtype=jnp.int32)
    wall = jnp.where((vertical_index == 0) | (vertical_index == height - 1), 0.0, 1.0).astype(jnp.float32)
    return jnp.concatenate([updated[:2], updated[2:3] * wall, updated[3:]], axis=0)

def pressure_source(provisional, mass, derivative, assemble):
    divergence = along_x(provisional[0:1], derivative) + along_y(provisional[1:2], derivative) + along_z(provisional[2:3], derivative)
    return -assemble(mass * divergence)

def apply_operator(field, mass, derivative, assemble):
    return assemble(stiffness_action(field, mass, derivative) + helmholtz_shift * mass * field)

def corrected_state(provisional, pressure, mass, counts, derivative, assemble):
    gradient = jnp.concatenate([along_x(pressure, derivative), along_y(pressure, derivative), along_z(pressure, derivative)], axis=0)
    velocity = provisional[:3] - assemble(mass * gradient) / (mass * counts)
    return jnp.concatenate([velocity, provisional[3:]], axis=0)

def inner_sum(first, second, counts):
    return jnp.sum(first * second / counts)

def reference(flow_state, building_height, pressure_old):
    gll_nodes, weights, derivative, eigen_basis, eigen_values = tables()
    first, width, depth, height = flow_state.shape
    mass = weight_grid(weights, width, depth, height)
    counts = multiplicity(width, depth, height)
    canopy = canopy_mask(building_height, height)
    across = interpolation(width, True, gll_nodes)
    along = interpolation(depth, True, gll_nodes)
    vertical = interpolation(height, False, gll_nodes)
    provisional = provisional_state(flow_state, mass, counts, canopy, derivative, assemble_global)
    source = pressure_source(provisional, mass, derivative, assemble_global)

    def operate(field):
        return apply_operator(field, mass, derivative, assemble_global)

    def smooth(residual):
        local = assemble_global(local_solve(residual, eigen_basis, eigen_values))
        coarse = prolong(coarse_solve(restrict(residual[0] / counts, across, along, vertical)), across, along, vertical)
        return local + coarse[None]
    pressure = pressure_old[None]
    residual = source - operate(pressure)
    smoothed = smooth(residual)
    direction = smoothed
    product = inner_sum(residual, smoothed, counts)
    for turn in range(ITERS):
        image = operate(direction)
        alpha = product / inner_sum(direction, image, counts)
        pressure = pressure + alpha * direction
        if turn + 1 < ITERS:
            residual = residual - alpha * image
            smoothed = smooth(residual)
            following = inner_sum(residual, smoothed, counts)
            direction = smoothed + following / product * direction
            product = following
    new_state = corrected_state(provisional, pressure, mass, counts, derivative, assemble_global)
    return (new_state, pressure[0])
```

```python
import math

import jax
import jax.numpy as jnp
import ml_dtypes
import numpy as np
from jax import lax
from jax.experimental import pallas as pl
from jax.experimental.pallas import tpu as pltpu
from jax.sharding import PartitionSpec as P

INTERPRET = False

viscosity = 0.05
time_step = 0.01
drag_strength = 20.0
heating = 40.0
buoyancy = 10.0
helmholtz_shift = 0.001
local_shift = 0.5
coarse_shift = 0.02
gll_points = (
    -1.0,
    -0.8717401485096066,
    -0.5917001814331423,
    -0.2092992179024789,
    0.2092992179024789,
    0.5917001814331423,
    0.8717401485096066,
    1.0,
)
EZ = 16
NZ = 128
NV = 17


def legendre_seven(points):
    squared = points * points
    return points * (((429.0 * squared - 693.0) * squared + 315.0) * squared - 35.0) / 16.0


def jacobi_eigen(matrix):
    current = np.array(matrix)
    basis = np.eye(8)
    for rounds in range(12):
        for first in range(7):
            for second in range(first + 1, 8):
                angle = 0.5 * math.atan2(
                    2.0 * float(current[first, second]),
                    float(current[second, second] - current[first, first]),
                )
                cosine = math.cos(angle)
                sine = math.sin(angle)
                rotation = np.eye(8)
                rotation[first, first] = cosine
                rotation[second, second] = cosine
                rotation[first, second] = sine
                rotation[second, first] = -sine
                current = rotation.T @ current @ rotation
                basis = basis @ rotation
    return (np.sum(current * np.eye(8), axis=0), basis)


def gll_tables():
    nodes = np.array(gll_points)
    values = legendre_seven(nodes)
    weights = 2.0 / (56.0 * values * values)
    differ = nodes[:, None] - nodes[None, :] + np.eye(8)
    derivative = values[:, None] / values[None, :] / differ * (1.0 - np.eye(8))
    ends = np.array([-14.0, 0.0, 0.0, 0.0, 0.0, 0.0, 0.0, 14.0])
    derivative = derivative + np.eye(8) * ends[None, :]
    stiffness = derivative.T @ (weights[:, None] * derivative)
    scaled = stiffness / np.sqrt(np.outer(weights, weights))
    scaled = 0.5 * (scaled + scaled.T)
    eigen_values, eigen_vectors = jacobi_eigen(scaled)
    eigen_basis = eigen_vectors / np.sqrt(weights)[:, None]
    return (nodes, weights, derivative, eigen_basis, np.maximum(eigen_values, 0.0))


def parts(table):
    table = np.asarray(table, np.float32)
    high = table.astype(ml_dtypes.bfloat16)
    low = (table - high.astype(np.float32)).astype(ml_dtypes.bfloat16)
    return high, low


def parts_three(table):
    high, low = parts(table)
    rest = np.asarray(table, np.float64) - high.astype(np.float64) - low.astype(np.float64)
    return high, low, rest.astype(ml_dtypes.bfloat16)


def left5(table):
    high, low, rest = parts_three(table)
    return np.concatenate([high, high, low, low, rest], axis=1)


def right5(table):
    high, low, rest = parts_three(table)
    return np.concatenate([high, high, low, low, rest], axis=0)


def left3(table):
    high, low = parts(table)
    return np.concatenate([high, high, low], axis=1)


def right3(table):
    high, low = parts(table)
    return np.concatenate([high, high, low], axis=0)


def split(field):
    high = field.astype(jnp.bfloat16)
    low = (field - high.astype(jnp.float32)).astype(jnp.bfloat16)
    return high, low


def stacked(field, terms, axis):
    high, low = split(field)
    order = [high, low, high, low, high] if terms == 5 else [high, low, high]
    return jnp.concatenate(order, axis=axis)


def lmul(table, field):
    terms = table.shape[1] // field.shape[0]
    return jnp.dot(table, stacked(field, terms, 0), preferred_element_type=jnp.float32)


def rmul(field, table):
    terms = table.shape[0] // field.shape[1]
    return jnp.dot(stacked(field, terms, 1), table, preferred_element_type=jnp.float32)


def lanes_of(field, size=64):
    return jnp.concatenate(
        [field[k * size : (k + 1) * size] for k in range(field.shape[0] // size)], axis=1
    )


def rows_of(field):
    return jnp.concatenate(
        [field[:, k * NZ : (k + 1) * NZ] for k in range(field.shape[1] // NZ)], axis=0
    )


def lane_index(rows):
    return lax.broadcasted_iota(jnp.int32, (rows, NZ), 1)


def turn(field, shift):
    return pltpu.roll(field, shift % NZ, 1)


def join_z(field):
    lane = lane_index(field.shape[0])
    ahead = jnp.where((lane % 8 == 7) & (lane < NZ - 1), turn(field, -1), 0.0)
    behind = jnp.where((lane % 8 == 0) & (lane > 0), turn(field, 1), 0.0)
    return field + ahead + behind


def join_x(rows, count):
    blocks = [rows[k * 64 : (k + 1) * 64] for k in range(count)]
    sums = [blocks[k][0:8] + blocks[(k - 1) % count][56:64] for k in range(count)]
    pieces = []
    for k in range(count):
        pieces += [sums[k], blocks[k][8:56], sums[(k + 1) % count]]
    return jnp.concatenate(pieces, axis=0)


def fold(field):
    return jnp.sum(field.reshape(field.shape[0] // 8, 8, NZ), axis=0)


def total(field):
    return jnp.sum(jnp.sum(field, axis=0, keepdims=True), axis=1, keepdims=True)


def tiled(table, count):
    return jnp.concatenate([table] * count, axis=0)


class Tables:
    def __init__(self, nx, ny):
        nodes, w, d, e, lam = gll_tables()
        self.nx, self.ny = nx, ny
        eye8 = np.eye(8)
        kx = d.T @ (w[:, None] * d)
        bx = np.diag(w)
        eyez = np.eye(EZ)
        join = np.eye(NZ)
        for k in range(EZ - 1):
            join[8 * k + 7, 8 * k + 8] = 1.0
            join[8 * k + 8, 8 * k + 7] = 1.0
        dz_t = np.kron(eyez, d).T
        kz_t = np.kron(eyez, kx).T
        wz = np.tile(w, EZ)
        wxy = np.kron(w, w)
        mz = join.sum(axis=1)
        m1 = np.array([2.0, 1, 1, 1, 1, 1, 1, 2.0])
        mxy = np.kron(m1, m1)
        f32 = np.float32
        mass = np.outer(wxy, wz)
        self.mass = mass.astype(f32)
        self.wz = np.broadcast_to(wz[None, :], (64, NZ)).astype(f32)
        self.wxy = np.broadcast_to(wxy[:, None], (64, NZ)).astype(f32)
        self.inv_bm = (1.0 / (mass * np.outer(mxy, mz))).astype(f32)
        self.inv_m = (1.0 / np.outer(mxy, mz)).astype(f32)
        self.inv_mz = np.broadcast_to(1.0 / mz[None, :], (64, NZ)).astype(f32)
        self.visc = np.stack([self.mass, self.wz, self.wxy]).reshape(192, NZ)
        dx = np.kron(d, eye8)
        dy = np.kron(eye8, d)
        lv = np.kron(kx, bx) + np.kron(bx, kx)
        self.k1_left = left5(np.concatenate([dx, dy, lv], axis=0))
        self.k1_right = right5(np.concatenate([dz_t, kz_t], axis=1))
        self.div_left = left5(np.concatenate([dx, dy], axis=1))
        self.dz_right = right5(dz_t)
        hx = np.stack([(1.0 - nodes) / 2.0, (1.0 + nodes) / 2.0])
        self.hx = hx
        hz = np.zeros((NZ, NV))
        for z in range(NZ):
            hz[z, z // 8] = hx[0, z % 8]
            hz[z, z // 8 + 1] = hx[1, z % 8]
        pxy = np.zeros((8, 64))
        for xv in range(2):
            for yv in range(2):
                pxy[xv * 2 + yv] = np.kron(hx[xv], hx[yv])
        self.pxy_left = left3(pxy)
        hzm = np.zeros((NZ, NZ))
        hzm[:, :NV] = hz / mz[:, None]
        self.hzm_right = right3(hzm)
        self.hy = np.broadcast_to(hx.reshape(16, 1), (16, NZ)).astype(f32)

        def hartley(count):
            angle = 2.0 * np.pi / count * np.outer(np.arange(count), np.arange(count))
            return (np.cos(angle) + np.sin(angle)) / np.sqrt(count)

        self.hart_x = hartley(nx)
        hart_y = hartley(ny)
        ex = 2.0 - 2.0 * np.cos(2.0 * np.pi / nx * np.arange(nx))
        ey = 2.0 - 2.0 * np.cos(2.0 * np.pi / ny * np.arange(ny))
        ez = 2.0 - 2.0 * np.cos(np.pi / NV * np.arange(NV))
        levels = np.arange(NV)
        norms = np.where(levels == 0, np.sqrt(1.0 / NV), np.sqrt(2.0 / NV))
        cz = np.cos(np.pi / NV * np.outer(levels + 0.5, levels)) * norms[None, :]
        inverse = 1.0 / (
            2.0 * (ex[:, None, None] + ey[None, :, None] + ez[None, None, :]) + coarse_shift
        )
        shifted = np.roll(hart_y, -1, axis=1)
        self.hart_cat = left3(np.concatenate([hart_y, shifted], axis=1))
        self.hart_two = left3(np.concatenate([hart_y, shifted], axis=0))
        hb = ny // 2
        self.hb = hb
        coef = np.zeros((nx * nx, NZ))
        for a in range(nx):
            for i in range(nx):
                for base in (0, 64):
                    coef[a * nx + i, base : base + NV] = self.hart_x[a, i]
                    coef[a * nx + i, base + NV : base + 2 * NV] = self.hart_x[a, (i + 1) % nx]
        self.coef = coef.astype(f32)
        twin = np.zeros((NZ, NZ))
        twin[:NV, :NV] = cz
        twin[64 : 64 + NV, 64 : 64 + NV] = cz
        self.twin_right = right3(twin)
        packed = np.zeros((nx, hb, NZ))
        packed[:, :, :NV] = inverse[:, :hb]
        packed[:, :, 64 : 64 + NV] = inverse[:, hb:]
        self.inv_packed = packed.reshape(nx * hb, NZ).astype(f32)
        near = np.zeros((ny, 16, hb))
        for j in range(ny):
            for yv in range(2):
                row = hart_y[(j + yv) % ny]
                near[j, yv] = row[:hb]
                near[j, 8 + yv] = row[hb:]
        self.near = np.stack([left3(block) for block in near])
        czh = np.zeros((NZ, NZ))
        czh[:NV] = (hz @ cz).T
        self.czh_right = right3(czh)
        self.et_left = left3(np.kron(e.T, e.T))
        self.e_left = left3(np.kron(e, e))
        self.et_right = right3(np.kron(eyez, e))
        self.e_right = right3(np.kron(eyez, e.T) @ join)
        lxy = (lam[:, None] + lam[None, :]).reshape(64)
        self.scale = (1.0 / (lxy[:, None] + np.tile(lam, EZ)[None, :] + local_shift)).astype(f32)
        self.a_left = left5(lv + helmholtz_shift * np.kron(bx, bx))
        self.a_right = right5(np.concatenate([wz[:, None] * join, kz_t @ join], axis=0))
        back = np.zeros((32, nx * 8))
        for yv in range(2):
            for a in range(nx):
                for i in range(nx):
                    back[yv * 16 + a, i * 8 : i * 8 + 8] = self.hart_x[a, i] * hx[yv]
        self.back_left = left3(back)
        hzc = np.zeros((NZ, NZ))
        hzc[:, :NV] = (hz / mz[:, None]) @ cz
        self.hzc_right = right3(hzc)
        self.edge_left = left3(np.concatenate([np.kron(eye8, d[:1]), np.kron(eye8, d[7:])], axis=0))
        wide = np.zeros((ny, nx, NZ))
        wide[:, :, :NV] = inverse.transpose(1, 0, 2)
        self.inv_wide = wide.reshape(ny, nx * NZ).astype(f32)
        around = np.zeros((ny, 8, ny))
        for j in range(ny):
            for yv in range(4):
                around[j, yv] = hart_y[(j + yv - 1) % ny]
        self.around = np.stack([left3(block) for block in around])
        reach = np.zeros((nx, 4, nx))
        for i in range(nx):
            for xv in range(4):
                reach[i, xv] = self.hart_x[(i + xv - 1) % nx]
        self.reach = reach.reshape(-1).astype(f32)
        second = np.diag(2.0 * np.ones(NV)) - np.eye(NV, k=1) - np.eye(NV, k=-1)
        second[0, 0] = second[-1, -1] = 1.0
        double = 2.0 * np.ones(NV)
        double[0] = double[-1] = 1.0
        mass_z = np.diag(double) - second / 3.0
        both = np.zeros((NZ, 2 * NZ))
        both[:NV, :NV] = cz.T @ mass_z @ cz
        both[:NV, NZ : NZ + NV] = cz.T @ (second / 2.0) @ cz
        self.galerkin_right = right3(both)
        self.mx = 2.0 - ex / 3.0
        self.kx = ex / 2.0
        my = np.broadcast_to((2.0 - ey / 3.0)[:, None], (ny, NZ))
        ky = np.broadcast_to((ey / 2.0)[:, None], (ny, NZ))
        self.mky = np.concatenate([my, ky], axis=0).astype(f32)
        self.last_left = left5(np.concatenate([dx, dy], axis=0))
        self.d = d


def call(kernel, outs, *args, scratch=(), smem=0):
    specs = [pl.BlockSpec(memory_space=pltpu.SMEM)] * smem
    specs += [pl.BlockSpec(memory_space=pltpu.VMEM)] * (len(args) - smem)
    return pl.pallas_call(
        kernel,
        out_shape=[jax.ShapeDtypeStruct(shape, jnp.float32) for shape in outs],
        in_specs=specs,
        out_specs=[pl.BlockSpec(memory_space=pltpu.VMEM)] * len(outs),
        scratch_shapes=list(scratch),
        interpret=INTERPRET,
        name=kernel.__name__,
    )(*args)


def stage_rate(h, flow, old, left, right, tab, fld, xf0, xf7, kp):
    f = [flow[q * 64 : q * 64 + 64] for q in range(4)]
    p = old[...]
    lx = lmul(left[...], jnp.concatenate(f + [p], axis=1))
    rx = rmul(jnp.concatenate(f + [p], axis=0), right[...])
    mass, wz, wxy = tab[0:64], tab[64:128], tab[128:192]
    u, v, w, theta = f
    drag = drag_strength * jnp.sqrt(u * u + v * v + w * w)
    canopy = (lane_index(64) // 8 < h[0, 0]).astype(jnp.float32)
    drag = drag * canopy
    forcing = [-drag * u, -drag * v, -drag * w + buoyancy * theta, heating * canopy]
    for q in range(5):
        lane = slice(q * NZ, q * NZ + NZ)
        rows = slice(q * 64, q * 64 + 64)
        gx, gy, lv = lx[0:64, lane], lx[64:128, lane], lx[128:192, lane]
        gz, kz = rx[rows, 0:NZ], rx[rows, NZ : 2 * NZ]
        stiff = lv * wz + wxy * kz
        if q < 4:
            rate = mass * (forcing[q] - (u * gx + v * gy + w * gz)) - viscosity * stiff
            fld[rows] = join_z(rate)
        else:
            kp[...] = stiff + helmholtz_shift * mass * p
            for k, grad in enumerate((gx, gy, gz)):
                fld[(4 + k) * 64 : (5 + k) * 64] = join_z(mass * grad)
    for q in range(7):
        xf0[q * 8 : q * 8 + 8] = fld[q * 64 : q * 64 + 8]
        xf7[q * 8 : q * 8 + 8] = fld[q * 64 + 56 : q * 64 + 64]


def stage_faces(fld, below, above, out, yf0, yf7):
    for q in range(7):
        base = q * 64
        out[base : base + 8] = fld[base : base + 8] + below[q * 8 : q * 8 + 8]
        out[base + 8 : base + 56] = fld[base + 8 : base + 56]
        out[base + 56 : base + 64] = fld[base + 56 : base + 64] + above[q * 8 : q * 8 + 8]
    yf0[...] = out[pl.ds(0, 56, stride=8), :]
    yf7[...] = out[pl.ds(7, 56, stride=8), :]


def add_faces(ref, below, above):
    count = ref.shape[0] // 8
    ref[pl.ds(0, count, stride=8), :] = ref[pl.ds(0, count, stride=8), :] + below
    ref[pl.ds(7, count, stride=8), :] = ref[pl.ds(7, count, stride=8), :] + above


def make_stages(t):
    nx, ny, hb = t.nx, t.ny, t.hb

    def stage_state(
        idx, fx, below, above, flow, kp, tab, dleft, dright, pleft, hright, prov, g0, rz, msg, scr
    ):
        scr[...] = fx[...]
        add_faces(scr, below[...], above[...])
        mass, inv_bm = tab[0:64], tab[64:128]
        lane = lane_index(64)
        new = []
        for q in range(4):
            rows = slice(q * 64, q * 64 + 64)
            value = flow[rows] + time_step * scr[rows] * inv_bm
            if q == 2:
                value = jnp.where((lane == 0) | (lane == NZ - 1), 0.0, value)
            prov[rows] = value
            new.append(value)
        for k in range(3):
            g0[k * 64 : k * 64 + 64] = scr[(4 + k) * 64 : (5 + k) * 64] * inv_bm
        div = lmul(dleft[...], jnp.concatenate(new[:2], axis=0)) + rmul(new[2], dright[...])
        joined = join_z(-mass * div - kp[...])
        rz[...] = joined
        coarse = rmul(lmul(pleft[...], joined), hright[...])
        face0 = rz[pl.ds(0, 8, stride=8), :]
        face7 = rz[pl.ds(7, 8, stride=8), :]
        for k in range(ny):
            msg[k * 16 : k * 16 + 8] = face0
            msg[k * 16 + 8 : k * 16 + 16] = coarse
        after = lax.rem(idx[1] + 1, ny)
        msg[pl.ds(pl.multiple_of(after * 16, 16), 8), :] = face7

    def stage_residual(idx, rec, rz, hart, out):
        out[0:64] = rz[...]
        before = lax.rem(idx[1] + ny - 1, ny)
        after = lax.rem(idx[1] + 1, ny)
        below = rec[pl.ds(pl.multiple_of(before * 16, 16), 8), :]
        above = rec[pl.ds(pl.multiple_of(after * 16, 16), 8), :]
        out[pl.ds(0, 8, stride=8), :] = out[pl.ds(0, 8, stride=8), :] + below
        out[pl.ds(7, 8, stride=8), :] = out[pl.ds(7, 8, stride=8), :] + above
        m = [rec[pl.ds(8 + r, ny, stride=16), :] for r in range(4)]
        top = m[0] + turn(m[2], NV)
        low = m[1] + turn(m[3], NV)
        modes = lmul(hart[...], jnp.concatenate([top, low], axis=0))
        out[64 : 64 + hb] = modes[0:hb] + turn(modes[hb:ny], 64)

    def smoothed(field, etl, etr, sc, er, el):
        modal = rmul(rows_of(lmul(etl, lanes_of(field))), etr)
        modal = rmul(modal * tiled(sc, nx), er)
        return rows_of(lmul(el, lanes_of(modal)))

    def stage_smooth(ring, etl, etr, sc, er, el, r0, s, s0, s7):
        size = 64 + hb
        rows = jnp.concatenate([ring[i * size : i * size + 64] for i in range(nx)], axis=0)
        residual = join_x(rows, nx)
        r0[...] = residual
        s[...] = join_x(smoothed(residual, etl[...], etr[...], sc[...], er[...], el[...]), nx)
        s0[...] = s[pl.ds(0, nx * 8, stride=8), :]
        s7[...] = s[pl.ds(7, nx * 8, stride=8), :]

    def stage_coarse(idx, ring, coef, twin, inv, near, czh, out):
        size = 64 + hb
        grid = [ring[i * size + 64 : (i + 1) * size] for i in range(nx)]
        modes = []
        for a in range(nx):
            acc = grid[0] * coef[a * nx : a * nx + 1]
            for i in range(1, nx):
                acc = acc + grid[i] * coef[a * nx + i : a * nx + i + 1]
            modes.append(acc + turn(acc, -NV))
        values = rmul(jnp.concatenate(modes, axis=0), twin[...]) * inv[...]
        pair = lmul(near[idx[1]], lanes_of(values, hb))
        lines = []
        for a in range(nx):
            tile = pair[:, a * NZ : (a + 1) * NZ]
            lines.append(tile[0:8] + turn(tile[8:16], 64))
        columns = []
        for i in range(nx):
            acc = lines[0] * float(t.hart_x[i, 0])
            for a in range(1, nx):
                acc = acc + lines[a] * float(t.hart_x[i, a])
            columns.append(acc)
        out[...] = rmul(jnp.concatenate(columns, axis=0), czh[...])

    def applied(field, al, wxy, ar):
        side = rows_of(lmul(al, lanes_of(field)))
        return rmul(jnp.concatenate([side, field * tiled(wxy, nx)], axis=1), ar)

    def restricted(field, back, hzc):
        columns = []
        for i in range(nx):
            acc = None
            for x in range(8):
                here = field[i * 64 + x * 8 : i * 64 + x * 8 + 8] * float(t.hx[0, x])
                k = (i - 1) % nx
                there = field[k * 64 + x * 8 : k * 64 + x * 8 + 8] * float(t.hx[1, x])
                acc = here + there if acc is None else acc + here + there
            columns.append(acc)
        return rmul(lmul(back, jnp.concatenate(columns, axis=0)), hzc)

    def stage_apply(
        s, below, above, vert, r0, hy, al, tab, ar, back, hzc, z0, q, q0, q7, cq, sums
    ):
        z0[...] = s[...]
        add_faces(z0, below[...], above[...])
        slabs = []
        for i in range(nx):
            slabs.append(
                hy[0:8] * vert[i * 8 : i * 8 + 1] + hy[8:16] * vert[i * 8 + 1 : i * 8 + 2]
            )
        pieces = []
        for i in range(nx):
            for x in range(8):
                pieces.append(
                    slabs[i] * float(t.hx[0, x]) + slabs[(i + 1) % nx] * float(t.hx[1, x])
                )
        field = z0[...] + jnp.concatenate(pieces, axis=0)
        z0[...] = field
        wxy, inv_m, inv_mz = tab[0:64], tab[64:128], tab[128:192]
        image = applied(field, al[...], wxy, ar[...])
        sums[0:8] = fold(r0[...] * field * tiled(inv_m, nx))
        sums[8:16] = fold(field * image * tiled(inv_mz, nx))
        cq[...] = restricted(image, back[...], hzc[...])
        q[...] = join_x(image, nx)
        q0[...] = q[pl.ds(0, nx * 8, stride=8), :]
        q7[...] = q[pl.ds(7, nx * 8, stride=8), :]

    def stage_again(q, below, above, tab, etl, etr, sc, er, el, s, s0, s7, sums, scr):
        scr[...] = q[...]
        add_faces(scr, below[...], above[...])
        field = scr[...]
        local = smoothed(field, etl[...], etr[...], sc[...], er[...], el[...])
        sums[...] = fold(field * local * tiled(tab[...], nx))
        s[...] = join_x(local, nx)
        s0[...] = s[pl.ds(0, nx * 8, stride=8), :]
        s7[...] = s[pl.ds(7, nx * 8, stride=8), :]

    def stage_gather(
        idx, s, below, above, z0, cq, sums1, sums2, al, tab, ar, back, hzc, edge, sq, msg, g0, g7
    ):
        sq[...] = s[...]
        add_faces(sq, below[...], above[...])
        field = sq[...]
        wxy, inv_mz = tab[0:64], tab[128:192]
        image = applied(field, al[...], wxy, ar[...])
        last = total(fold(field * image * tiled(inv_mz, nx)))
        tq = restricted(image, back[...], hzc[...])
        block = cq[0:16] + turn(cq[16:32], 32) + turn(tq[0:16], 64) + turn(tq[16:32], 96)
        lane = lane_index(16)
        row = lax.broadcasted_iota(jnp.int32, (16, NZ), 0)
        values = [total(sums1[0:8]), total(sums1[8:16]), total(sums2[...]), last]
        for k, value in enumerate(values):
            block = block + jnp.where((row == 12) & (lane == NV + k), value, 0.0)
        for k in range(ny):
            msg[k * 16 : k * 16 + 16] = block
        base = pl.multiple_of(idx[0] * 64, 64)
        pair = jnp.concatenate([z0[pl.ds(base, 64), :], sq[pl.ds(base, 64), :]], axis=1)
        slopes = lmul(edge[...], pair)
        g0[...] = jnp.concatenate([slopes[0:8, 0:NZ], slopes[0:8, NZ:]], axis=0)
        g7[...] = jnp.concatenate([slopes[8:16, 0:NZ], slopes[8:16, NZ:]], axis=0)

    def stage_final(
        idx,
        reach,
        rec,
        below,
        above,
        z0,
        sq,
        prov,
        g0,
        old,
        hart,
        inv,
        around,
        czh,
        gal,
        mky,
        hy,
        left,
        right,
        inv_mz,
        new,
        press,
        scr,
    ):
        cells = jnp.concatenate([rec[pl.ds(a, ny, stride=16), :] for a in range(nx)], axis=1)
        both = lmul(hart[...], cells)
        my, ky = mky[0:ny], mky[ny : 2 * ny]
        lane = lane_index(ny)
        found = []
        cross = jnp.zeros((ny, NZ), jnp.float32)
        plain = jnp.zeros((ny, NZ), jnp.float32)
        for a in range(nx):
            tile = slice(a * NZ, (a + 1) * NZ)
            comb = both[0:ny, tile] + turn(both[ny : 2 * ny, tile], -32)
            e = comb * inv[:, tile]
            found.append(e)
            plain = plain + e * comb
            cross = cross + e * turn(comb, -64)
        grown = rmul(jnp.concatenate(found, axis=0), gal[...])
        quad = jnp.zeros((ny, NZ), jnp.float32)
        for a in range(nx):
            rows = slice(a * ny, (a + 1) * ny)
            mxa, kxa = float(t.mx[a]), float(t.kx[a])
            weight_m = my * (kxa + helmholtz_shift * mxa) + ky * mxa
            weight_k = my * mxa
            quad = quad + found[a] * (
                weight_m * grown[rows, 0:NZ] + weight_k * grown[rows, NZ : 2 * NZ]
            )
        scalars = jnp.sum(rec[pl.ds(12, ny, stride=16), :], axis=0, keepdims=True)
        line = lane_index(1)

        def pick(k):
            return jnp.sum(jnp.where(line == NV + k, scalars, 0.0), axis=1, keepdims=True)

        rz0, zq0 = pick(0), pick(1)
        wq = pick(2) + total(plain)
        ww = pick(3) + 2.0 * total(cross) + total(quad)
        first = rz0 / zq0
        rz1 = rz0 - 2.0 * first * zq0 + first * first * wq
        beta = rz1 / rz0
        grow = 1.0 + beta
        curve = grow * grow * zq0 - 2.0 * grow * first * wq + first * first * ww
        second = rz1 / curve
        on_z = first + second * grow
        on_w = -second * first
        lines = lmul(around[idx[1]], jnp.concatenate(found, axis=1))
        stack = []
        for xv in range(4):
            base = (idx[0] * 4 + xv) * nx
            acc = lines[:, 0:NZ] * reach[base]
            for a in range(1, nx):
                acc = acc + lines[:, a * NZ : (a + 1) * NZ] * reach[base + a]
            stack.append(acc)
        scr[...] = rmul(jnp.concatenate(stack, axis=0), czh[...]) * on_w
        hy0, hy1 = hy[0:8], hy[8:16]
        slabs = [hy0 * scr[k * 8 + 1 : k * 8 + 2] + hy1 * scr[k * 8 + 2 : k * 8 + 3] for k in range(4)]
        coarse = jnp.concatenate(
            [slabs[1] * float(t.hx[0, x]) + slabs[2] * float(t.hx[1, x]) for x in range(8)], axis=0
        )

        def own(shift):
            base = pl.multiple_of(lax.rem(idx[0] + shift + nx, nx) * 64, 64)
            return z0[pl.ds(base, 64), :] * on_z + sq[pl.ds(base, 64), :] * on_w

        change = own(0) + coarse
        press[...] = old[...] + change
        slopes = lmul(left[...], change)
        gx, gy = slopes[0:64], slopes[64:128]
        gz = rmul(change, right[...])
        prior, later = own(-1), own(1)
        edge0 = 0.5 * (slabs[1] - slabs[0])
        edge7 = 0.5 * (slabs[3] - slabs[2])
        for x in range(8):
            edge0 = edge0 + prior[x * 8 : x * 8 + 8] * float(t.d[7, x])
            edge7 = edge7 + later[x * 8 : x * 8 + 8] * float(t.d[0, x])
        new[0:8] = prov[0:8] - g0[0:8] - 0.5 * (gx[0:8] + edge0)
        new[8:56] = prov[8:56] - g0[8:56] - gx[8:56]
        new[56:64] = prov[56:64] - g0[56:64] - 0.5 * (gx[56:64] + edge7)
        hx0, hx1 = hy0, hy1
        line1 = [scr[k * 8 + 1 : k * 8 + 2] for k in range(4)]
        step0 = [0.5 * (scr[k * 8 + 1 : k * 8 + 2] - scr[k * 8 : k * 8 + 1]) for k in (1, 2)]
        step7 = [0.5 * (scr[k * 8 + 3 : k * 8 + 4] - scr[k * 8 + 2 : k * 8 + 3]) for k in (1, 2)]
        under = below[0:8] * on_z + below[8:16] * on_w + hx0 * step0[0] + hx1 * step0[1]
        over = above[0:8] * on_z + above[8:16] * on_w + hx0 * step7[0] + hx1 * step7[1]
        press_y = gy
        new[64:128] = press_y
        own0 = new[pl.ds(64, 8, stride=8), :]
        own7 = new[pl.ds(71, 8, stride=8), :]
        new[pl.ds(64, 8, stride=8), :] = 0.5 * (own0 + under)
        new[pl.ds(71, 8, stride=8), :] = 0.5 * (own7 + over)
        new[64:128] = prov[64:128] - g0[64:128] - new[64:128]
        new[128:192] = prov[128:192] - g0[128:192] - join_z(gz) * inv_mz[...]
        new[192:256] = prov[192:256]

    return (
        stage_state,
        stage_residual,
        stage_smooth,
        stage_coarse,
        stage_apply,
        stage_again,
        stage_gather,
        stage_final,
    )


def exchange(axis, first, last):
    count = lax.axis_size(axis)
    below = lax.ppermute(last, axis, [(k, (k + 1) % count) for k in range(count)])
    above = lax.ppermute(first, axis, [((k + 1) % count, k) for k in range(count)])
    return below, above


def make_device(t):
    nx, ny, hb = t.nx, t.ny, t.hb
    (
        stage_state,
        stage_residual,
        stage_smooth,
        stage_coarse,
        stage_apply,
        stage_again,
        stage_gather,
        stage_final,
    ) = make_stages(t)
    c = jnp.asarray
    col, ring, face = (64, NZ), (nx * 64, NZ), (nx * 8, NZ)

    def on_device(flow_state, building_height, pressure_old):
        flow = flow_state.reshape(256, NZ)
        old = pressure_old.reshape(64, NZ)
        idx = jnp.stack([lax.axis_index("gx"), lax.axis_index("gy")]).astype(jnp.int32)
        fld, xf0, xf7, kp = call(
            stage_rate,
            [(448, NZ), (56, NZ), (56, NZ), col],
            building_height,
            flow,
            old,
            c(t.k1_left),
            c(t.k1_right),
            c(t.visc),
            smem=1,
        )
        below, above = exchange("gx", xf0, xf7)
        fld, yf0, yf7 = call(
            stage_faces, [(448, NZ), (56, NZ), (56, NZ)], fld, below, above
        )
        below, above = exchange("gy", yf0, yf7)
        prov, g0, rz, msg = call(
            stage_state,
            [(256, NZ), (192, NZ), col, (ny * 16, NZ)],
            idx,
            fld,
            below,
            above,
            flow,
            kp,
            c(np.concatenate([t.mass, t.inv_bm])),
            c(t.div_left),
            c(t.dz_right),
            c(t.pxy_left),
            c(t.hzm_right),
            smem=1,
            scratch=[pltpu.VMEM((448, NZ), jnp.float32)],
        )
        rec = lax.all_to_all(msg.reshape(ny, 16, NZ), "gy", 0, 0, tiled=True)
        (piece,) = call(
            stage_residual,
            [(64 + hb, NZ)],
            idx,
            rec.reshape(ny * 16, NZ),
            rz,
            c(t.hart_cat),
            smem=1,
        )
        whole = lax.all_gather(piece, "gx", axis=0, tiled=True)
        smoother = (c(t.et_left), c(t.et_right), c(t.scale), c(t.e_right), c(t.e_left))
        r0, s, s0, s7 = call(stage_smooth, [ring, ring, face, face], whole, *smoother)
        below, above = exchange("gy", s0, s7)
        (vert,) = call(
            stage_coarse,
            [face],
            idx,
            whole,
            c(t.coef),
            c(t.twin_right),
            c(t.inv_packed),
            c(t.near),
            c(t.czh_right),
            smem=1,
        )
        tab = c(np.concatenate([t.wxy, t.inv_m, t.inv_mz]))
        operator = (c(t.a_left), tab, c(t.a_right), c(t.back_left), c(t.hzc_right))
        z0, q, q0, q7, cq, sums1 = call(
            stage_apply,
            [ring, ring, face, face, (32, NZ), (16, NZ)],
            s,
            below,
            above,
            vert,
            r0,
            c(t.hy),
            *operator,
        )
        below, above = exchange("gy", q0, q7)
        s, s0, s7, sums2 = call(
            stage_again,
            [ring, face, face, (8, NZ)],
            q,
            below,
            above,
            c(t.inv_mz),
            *smoother,
            scratch=[pltpu.VMEM(ring, jnp.float32)],
        )
        below, above = exchange("gy", s0, s7)
        sq, msg, e0, e7 = call(
            stage_gather,
            [ring, (ny * 16, NZ), (16, NZ), (16, NZ)],
            idx,
            s,
            below,
            above,
            z0,
            cq,
            sums1,
            sums2,
            *operator,
            c(t.edge_left),
            smem=1,
        )
        below, above = exchange("gy", e0, e7)
        rec = lax.all_to_all(msg.reshape(ny, 16, NZ), "gy", 0, 0, tiled=True)
        new, press = call(
            stage_final,
            [(256, NZ), col],
            idx,
            c(t.reach),
            rec.reshape(ny * 16, NZ),
            below,
            above,
            z0,
            sq,
            prov,
            g0,
            old,
            c(t.hart_two),
            c(t.inv_wide),
            c(t.around),
            c(t.czh_right),
            c(t.galerkin_right),
            c(t.mky),
            c(t.hy),
            c(t.last_left),
            c(t.dz_right),
            c(t.inv_mz),
            smem=2,
            scratch=[pltpu.VMEM((32, NZ), jnp.float32)],
        )
        return new.reshape(flow_state.shape), press.reshape(pressure_old.shape)

    return on_device


def solution(mesh):
    t = Tables(mesh.shape["gx"], mesh.shape["gy"])
    in_specs = (P(None, "gx", "gy", None), P("gx", "gy"), P("gx", "gy", None))
    out_specs = (P(None, "gx", "gy", None), P("gx", "gy", None))
    return jax.shard_map(
        make_device(t), mesh=mesh, in_specs=in_specs, out_specs=out_specs, check_vma=False
    )
```

```python
import math

import jax
import jax.numpy as jnp
import ml_dtypes
import numpy as np
from jax import lax
from jax.experimental import pallas as pl
from jax.experimental.pallas import tpu as pltpu
from jax.sharding import PartitionSpec as P

INTERPRET = False
VMEM_LIMIT = 16 * 1024 * 1024

viscosity = 0.05
time_step = 0.01
drag_strength = 20.0
heating = 40.0
buoyancy = 10.0
helmholtz_shift = 0.001
local_shift = 0.5
coarse_shift = 0.02
gll_points = (
    -1.0,
    -0.8717401485096066,
    -0.5917001814331423,
    -0.2092992179024789,
    0.2092992179024789,
    0.5917001814331423,
    0.8717401485096066,
    1.0,
)
EZ = 16
NZ = 128
NV = 17


def legendre_seven(points):
    squared = points * points
    return points * (((429.0 * squared - 693.0) * squared + 315.0) * squared - 35.0) / 16.0


def jacobi_eigen(matrix):
    current = np.array(matrix)
    basis = np.eye(8)
    for rounds in range(12):
        for first in range(7):
            for second in range(first + 1, 8):
                angle = 0.5 * math.atan2(
                    2.0 * float(current[first, second]),
                    float(current[second, second] - current[first, first]),
                )
                cosine = math.cos(angle)
                sine = math.sin(angle)
                rotation = np.eye(8)
                rotation[first, first] = cosine
                rotation[second, second] = cosine
                rotation[first, second] = sine
                rotation[second, first] = -sine
                current = rotation.T @ current @ rotation
                basis = basis @ rotation
    return (np.sum(current * np.eye(8), axis=0), basis)


def gll_tables():
    nodes = np.array(gll_points)
    values = legendre_seven(nodes)
    weights = 2.0 / (56.0 * values * values)
    differ = nodes[:, None] - nodes[None, :] + np.eye(8)
    derivative = values[:, None] / values[None, :] / differ * (1.0 - np.eye(8))
    ends = np.array([-14.0, 0.0, 0.0, 0.0, 0.0, 0.0, 0.0, 14.0])
    derivative = derivative + np.eye(8) * ends[None, :]
    stiffness = derivative.T @ (weights[:, None] * derivative)
    scaled = stiffness / np.sqrt(np.outer(weights, weights))
    scaled = 0.5 * (scaled + scaled.T)
    eigen_values, eigen_vectors = jacobi_eigen(scaled)
    eigen_basis = eigen_vectors / np.sqrt(weights)[:, None]
    return (nodes, weights, derivative, eigen_basis, np.maximum(eigen_values, 0.0))


def parts(table):
    table = np.asarray(table, np.float32)
    high = table.astype(ml_dtypes.bfloat16)
    low = (table - high.astype(np.float32)).astype(ml_dtypes.bfloat16)
    return high, low


def parts_three(table):
    high, low = parts(table)
    rest = np.asarray(table, np.float64) - high.astype(np.float64) - low.astype(np.float64)
    return high, low, rest.astype(ml_dtypes.bfloat16)


def left5(table):
    high, low, rest = parts_three(table)
    return np.concatenate([high, high, low, low, rest], axis=1)


def right5(table):
    return np.concatenate(parts_three(table), axis=0)


def left3(table):
    high, low = parts(table)
    return np.concatenate([high, high, low], axis=1)


def right3(table):
    return np.concatenate(parts(table), axis=0)


def split(field):
    high = field.astype(jnp.bfloat16)
    low = (field - high.astype(jnp.float32)).astype(jnp.bfloat16)
    return high, low


def stacked(field, terms, axis):
    high, low = split(field)
    order = [high, low, high, low, high] if terms == 5 else [high, low, high]
    return jnp.concatenate(order, axis=axis)


def lmul(table, field):
    terms = table.shape[1] // field.shape[0]
    return jnp.dot(table, stacked(field, terms, 0), preferred_element_type=jnp.float32)


def rmul(field, table):
    size = field.shape[1]
    part = [table[k : k + size] for k in range(0, table.shape[0], size)]
    order = [part[0], part[0], part[1], part[1], part[2]] if len(part) == 3 else [part[0]] + part
    return jnp.dot(
        stacked(field, len(order), 1),
        jnp.concatenate(order, axis=0),
        preferred_element_type=jnp.float32,
    )


def thrice(table, field):
    high, low = split(table)
    first, second = split(field)
    out = jnp.dot(high, first, preferred_element_type=jnp.float32)
    out = out + jnp.dot(high, second, preferred_element_type=jnp.float32)
    return out + jnp.dot(low, first, preferred_element_type=jnp.float32)


def lanes_of(field, size=64):
    return jnp.concatenate(
        [field[k * size : (k + 1) * size] for k in range(field.shape[0] // size)], axis=1
    )


def rows_of(field):
    return jnp.concatenate(
        [field[:, k * NZ : (k + 1) * NZ] for k in range(field.shape[1] // NZ)], axis=0
    )


def lane_index(rows):
    return lax.broadcasted_iota(jnp.int32, (rows, NZ), 1)


def turn(field, shift):
    return pltpu.roll(field, shift % NZ, 1)


def join_z(field):
    lane = lane_index(field.shape[0])
    ahead = jnp.where((lane % 8 == 7) & (lane < NZ - 1), turn(field, -1), 0.0)
    behind = jnp.where((lane % 8 == 0) & (lane > 0), turn(field, 1), 0.0)
    return field + ahead + behind


def join_x(rows, count):
    blocks = [rows[k * 64 : (k + 1) * 64] for k in range(count)]
    sums = [blocks[k][0:8] + blocks[(k - 1) % count][56:64] for k in range(count)]
    pieces = []
    for k in range(count):
        pieces += [sums[k], blocks[k][8:56], sums[(k + 1) % count]]
    return jnp.concatenate(pieces, axis=0)


def fold(field):
    return jnp.sum(field.reshape(field.shape[0] // 8, 8, NZ), axis=0)


def total(field):
    return jnp.sum(jnp.sum(field, axis=0, keepdims=True), axis=1, keepdims=True)


def tiled(table, count):
    return jnp.concatenate([table] * count, axis=0)


class Tables:
    def __init__(self, nx, ny):
        nodes, w, d, e, lam = gll_tables()
        self.nx, self.ny = nx, ny
        eye8 = np.eye(8)
        kx = d.T @ (w[:, None] * d)
        bx = np.diag(w)
        eyez = np.eye(EZ)
        join = np.eye(NZ)
        for k in range(EZ - 1):
            join[8 * k + 7, 8 * k + 8] = 1.0
            join[8 * k + 8, 8 * k + 7] = 1.0
        dz_t = np.kron(eyez, d).T
        kz_t = np.kron(eyez, kx).T
        wz = np.tile(w, EZ)
        wxy = np.kron(w, w)
        mz = join.sum(axis=1)
        m1 = np.array([2.0, 1, 1, 1, 1, 1, 1, 2.0])
        mxy = np.kron(m1, m1)
        f32 = np.float32
        mass = np.outer(wxy, wz)
        self.mass = mass.astype(f32)
        self.wz = np.broadcast_to(wz[None, :], (64, NZ)).astype(f32)
        self.wxy = np.broadcast_to(wxy[:, None], (64, NZ)).astype(f32)
        self.inv_bm = (1.0 / (mass * np.outer(mxy, mz))).astype(f32)
        self.inv_m = (1.0 / np.outer(mxy, mz)).astype(f32)
        self.inv_mz = np.broadcast_to(1.0 / mz[None, :], (64, NZ)).astype(f32)
        self.visc = np.stack([self.mass, self.wz, self.wxy]).reshape(192, NZ)
        dx = np.kron(d, eye8)
        dy = np.kron(eye8, d)
        lv = np.kron(kx, bx) + np.kron(bx, kx)
        self.k1_left = left5(np.concatenate([dx, dy, lv], axis=0))
        self.k1_right = right5(np.concatenate([dz_t, kz_t], axis=1))
        self.div_left = left5(np.concatenate([dx, dy], axis=1))
        self.dz_right = right5(dz_t)
        hx = np.stack([(1.0 - nodes) / 2.0, (1.0 + nodes) / 2.0])
        self.hx = hx
        hz = np.zeros((NZ, NV))
        for z in range(NZ):
            hz[z, z // 8] = hx[0, z % 8]
            hz[z, z // 8 + 1] = hx[1, z % 8]
        pxy = np.zeros((8, 64))
        for xv in range(2):
            for yv in range(2):
                pxy[xv * 2 + yv] = np.kron(hx[xv], hx[yv])
        self.pxy_left = left3(pxy)
        hzm = np.zeros((NZ, NZ))
        hzm[:, :NV] = hz / mz[:, None]
        self.hzm_right = right3(hzm)
        self.hy = np.broadcast_to(hx.reshape(16, 1), (16, NZ)).astype(f32)

        def hartley(count):
            angle = 2.0 * np.pi / count * np.outer(np.arange(count), np.arange(count))
            return (np.cos(angle) + np.sin(angle)) / np.sqrt(count)

        self.hart_x = hartley(nx)
        hart_y = hartley(ny)
        ex = 2.0 - 2.0 * np.cos(2.0 * np.pi / nx * np.arange(nx))
        ey = 2.0 - 2.0 * np.cos(2.0 * np.pi / ny * np.arange(ny))
        ez = 2.0 - 2.0 * np.cos(np.pi / NV * np.arange(NV))
        levels = np.arange(NV)
        norms = np.where(levels == 0, np.sqrt(1.0 / NV), np.sqrt(2.0 / NV))
        cz = np.cos(np.pi / NV * np.outer(levels + 0.5, levels)) * norms[None, :]
        inverse = 1.0 / (
            2.0 * (ex[:, None, None] + ey[None, :, None] + ez[None, None, :]) + coarse_shift
        )
        shifted = np.roll(hart_y, -1, axis=1)
        self.hart_cat = left3(np.concatenate([hart_y, shifted], axis=1))
        self.hart_two = left3(np.concatenate([hart_y, shifted], axis=0))
        hb = ny // 2
        self.hb = hb
        coef = np.zeros((nx * nx, NZ))
        for a in range(nx):
            for i in range(nx):
                for base in (0, 64):
                    coef[a * nx + i, base : base + NV] = self.hart_x[a, i]
                    coef[a * nx + i, base + NV : base + 2 * NV] = self.hart_x[a, (i + 1) % nx]
        self.coef = coef.astype(f32)
        twin = np.zeros((NZ, NZ))
        twin[:NV, :NV] = cz
        twin[64 : 64 + NV, 64 : 64 + NV] = cz
        self.twin_right = right3(twin)
        packed = np.zeros((nx, hb, NZ))
        packed[:, :, :NV] = inverse[:, :hb]
        packed[:, :, 64 : 64 + NV] = inverse[:, hb:]
        self.inv_packed = packed.reshape(nx * hb, NZ).astype(f32)
        near = hart_y[(np.arange(ny + 8) - 1) % ny]
        self.near = near.astype(f32)
        self.near_low = near[:, :hb].astype(f32)
        self.near_high = near[:, hb:].astype(f32)
        czh = np.zeros((NZ, NZ))
        czh[:NV] = (hz @ cz).T
        self.czh_right = right3(czh)
        self.et_left = left3(np.kron(e.T, e.T))
        self.e_left = left3(np.kron(e, e))
        self.et_right = right3(np.kron(eyez, e))
        self.e_right = right3(np.kron(eyez, e.T) @ join)
        lxy = (lam[:, None] + lam[None, :]).reshape(64)
        self.scale = (1.0 / (lxy[:, None] + np.tile(lam, EZ)[None, :] + local_shift)).astype(f32)
        self.a_left = left5(lv + helmholtz_shift * np.kron(bx, bx))
        self.a_right = right5(np.concatenate([wz[:, None] * join, kz_t @ join], axis=0))
        back = np.zeros((32, nx * 8))
        for yv in range(2):
            for a in range(nx):
                for i in range(nx):
                    back[yv * 16 + a, i * 8 : i * 8 + 8] = self.hart_x[a, i] * hx[yv]
        self.back_left = left3(back)
        hzc = np.zeros((NZ, NZ))
        hzc[:, :NV] = (hz / mz[:, None]) @ cz
        self.hzc_right = right3(hzc)
        self.edge_left = left3(np.concatenate([np.kron(eye8, d[:1]), np.kron(eye8, d[7:])], axis=0))
        self.ex = ex
        ez_row = np.zeros((8, NZ))
        ez_row[:, :NV] = ez
        self.ez_row = ez_row.astype(f32)
        reach = np.zeros((nx, 4, nx))
        for i in range(nx):
            for xv in range(4):
                reach[i, xv] = self.hart_x[(i + xv - 1) % nx]
        self.reach = reach.reshape(-1).astype(f32)
        second = np.diag(2.0 * np.ones(NV)) - np.eye(NV, k=1) - np.eye(NV, k=-1)
        second[0, 0] = second[-1, -1] = 1.0
        double = 2.0 * np.ones(NV)
        double[0] = double[-1] = 1.0
        mass_z = np.diag(double) - second / 3.0
        both = np.zeros((NZ, 2 * NZ))
        both[:NV, :NV] = cz.T @ mass_z @ cz
        both[:NV, NZ : NZ + NV] = cz.T @ (second / 2.0) @ cz
        self.galerkin_right = right3(both)
        self.mx = 2.0 - ex / 3.0
        self.kx = ex / 2.0
        my = np.broadcast_to((2.0 - ey / 3.0)[:, None], (ny, NZ))
        ky = np.broadcast_to((ey / 2.0)[:, None], (ny, NZ))
        self.mky = np.concatenate([my, ky], axis=0).astype(f32)
        self.last_left = left5(np.concatenate([dx, dy], axis=0))
        self.d = d


def call(kernel, outs, *args, scratch=(), smem=0):
    specs = [pl.BlockSpec(memory_space=pltpu.SMEM)] * smem
    specs += [pl.BlockSpec(memory_space=pltpu.VMEM)] * (len(args) - smem)
    return pl.pallas_call(
        kernel,
        out_shape=[jax.ShapeDtypeStruct(shape, jnp.float32) for shape in outs],
        in_specs=specs,
        out_specs=[pl.BlockSpec(memory_space=pltpu.VMEM)] * len(outs),
        scratch_shapes=list(scratch),
        interpret=INTERPRET,
        compiler_params=pltpu.CompilerParams(vmem_limit_bytes=VMEM_LIMIT),
        name=kernel.__name__,
    )(*args)


def stage_rate(idx, h, flow, old, left, right, tab, fld, xa, xb, kp):
    f = [flow[q * 64 : q * 64 + 64] for q in range(4)]
    p = old[...]
    lx = lmul(left[...], jnp.concatenate(f + [p], axis=1))
    rx = rmul(jnp.concatenate(f + [p], axis=0), right[...])
    mass, wz, wxy = tab[0:64], tab[64:128], tab[128:192]
    u, v, w, theta = f
    drag = drag_strength * jnp.sqrt(u * u + v * v + w * w)
    canopy = (lane_index(64) // 8 < h[0, 0]).astype(jnp.float32)
    drag = drag * canopy
    forcing = [-drag * u, -drag * v, -drag * w + buoyancy * theta, heating * canopy]
    for q in range(5):
        lane = slice(q * NZ, q * NZ + NZ)
        rows = slice(q * 64, q * 64 + 64)
        gx, gy, lv = lx[0:64, lane], lx[64:128, lane], lx[128:192, lane]
        gz, kz = rx[rows, 0:NZ], rx[rows, NZ : 2 * NZ]
        stiff = lv * wz + wxy * kz
        if q < 4:
            rate = mass * (forcing[q] - (u * gx + v * gy + w * gz)) - viscosity * stiff
            fld[rows] = join_z(rate)
        else:
            kp[...] = stiff + helmholtz_shift * mass * p
            for k, grad in enumerate((gx, gy, gz)):
                fld[(4 + k) * 64 : (5 + k) * 64] = join_z(mass * grad)
    start = jnp.concatenate([fld[q * 64 : q * 64 + 8] for q in range(7)], axis=0)
    end = jnp.concatenate([fld[q * 64 + 56 : q * 64 + 64] for q in range(7)], axis=0)
    swap_out(is_odd(idx[0]), start, end, xa, xb)


def stage_faces(idx, fld, xa, xb, out, ya, yb):
    below, above = swap_in(is_odd(idx[0]), xa, xb)
    for q in range(7):
        base = q * 64
        out[base : base + 8] = fld[base : base + 8] + below[q * 8 : q * 8 + 8]
        out[base + 8 : base + 56] = fld[base + 8 : base + 56]
        out[base + 56 : base + 64] = fld[base + 56 : base + 64] + above[q * 8 : q * 8 + 8]
    swap_faces(is_odd(idx[1]), out, ya, yb)


def swap_faces(odd, ref, first, second):
    count = ref.shape[0] // 8
    start = ref[pl.ds(0, count, stride=8), :]
    end = ref[pl.ds(7, count, stride=8), :]
    swap_out(odd, start, end, first, second)


def add_faces(odd, ref, first, second):
    below, above = swap_in(odd, first, second)
    count = ref.shape[0] // 8
    ref[pl.ds(0, count, stride=8), :] = ref[pl.ds(0, count, stride=8), :] + below
    ref[pl.ds(7, count, stride=8), :] = ref[pl.ds(7, count, stride=8), :] + above


def swap_out(odd, start, end, first, second):
    first[...] = jnp.where(odd, start, end)
    second[...] = jnp.where(odd, end, start)


def swap_in(odd, first, second):
    return jnp.where(odd, first[...], second[...]), jnp.where(odd, second[...], first[...])


def is_odd(index):
    return lax.rem(index, 2) == 1


def make_stages(t):
    nx, ny, hb = t.nx, t.ny, t.hb

    def stage_state(
        idx, fx, below, above, flow, kp, tab, dleft, dright, pleft, hright, prov, g0, rz, msg, scr
    ):
        scr[...] = fx[...]
        add_faces(is_odd(idx[1]), scr, below, above)
        mass, inv_bm = tab[0:64], tab[64:128]
        lane = lane_index(64)
        new = []
        for q in range(4):
            rows = slice(q * 64, q * 64 + 64)
            value = flow[rows] + time_step * scr[rows] * inv_bm
            if q == 2:
                value = jnp.where((lane == 0) | (lane == NZ - 1), 0.0, value)
            prov[rows] = value
            new.append(value)
        for k in range(3):
            g0[k * 64 : k * 64 + 64] = scr[(4 + k) * 64 : (5 + k) * 64] * inv_bm
        div = lmul(dleft[...], jnp.concatenate(new[:2], axis=0)) + rmul(new[2], dright[...])
        joined = join_z(-mass * div - kp[...])
        rz[...] = joined
        coarse = rmul(lmul(pleft[...], joined), hright[...])
        face0 = rz[pl.ds(0, 8, stride=8), :]
        face7 = rz[pl.ds(7, 8, stride=8), :]
        for k in range(ny):
            msg[k * 16 : k * 16 + 8] = face0
            msg[k * 16 + 8 : k * 16 + 16] = coarse
        after = lax.rem(idx[1] + 1, ny)
        msg[pl.ds(pl.multiple_of(after * 16, 16), 8), :] = face7

    def stage_residual(idx, rec, rz, hart, out):
        out[0:64] = rz[...]
        before = lax.rem(idx[1] + ny - 1, ny)
        after = lax.rem(idx[1] + 1, ny)
        below = rec[pl.ds(pl.multiple_of(before * 16, 16), 8), :]
        above = rec[pl.ds(pl.multiple_of(after * 16, 16), 8), :]
        out[pl.ds(0, 8, stride=8), :] = out[pl.ds(0, 8, stride=8), :] + below
        out[pl.ds(7, 8, stride=8), :] = out[pl.ds(7, 8, stride=8), :] + above
        m = [rec[pl.ds(8 + r, ny, stride=16), :] for r in range(4)]
        top = m[0] + turn(m[2], NV)
        low = m[1] + turn(m[3], NV)
        modes = lmul(hart[...], jnp.concatenate([top, low], axis=0))
        out[64 : 64 + hb] = modes[0:hb] + turn(modes[hb:ny], 64)

    def smoothed(field, etl, etr, sc, er, el):
        modal = rmul(rows_of(lmul(etl, lanes_of(field))), etr)
        modal = rmul(modal * tiled(sc, nx), er)
        return rows_of(lmul(el, lanes_of(modal)))

    def stage_smooth(idx, ring, etl, etr, sc, er, el, r0, s, s0, s7):
        size = 64 + hb
        rows = jnp.concatenate([ring[i * size : i * size + 64] for i in range(nx)], axis=0)
        residual = join_x(rows, nx)
        r0[...] = residual
        s[...] = join_x(smoothed(residual, etl[...], etr[...], sc[...], er[...], el[...]), nx)
        swap_faces(is_odd(idx[1]), s, s0, s7)

    def stage_coarse(idx, ring, coef, twin, inv, near_low, near_high, czh, out):
        size = 64 + hb
        grid = [ring[i * size + 64 : (i + 1) * size] for i in range(nx)]
        modes = []
        for a in range(nx):
            acc = grid[0] * coef[a * nx : a * nx + 1]
            for i in range(1, nx):
                acc = acc + grid[i] * coef[a * nx + i : a * nx + i + 1]
            modes.append(acc + turn(acc, -NV))
        values = rmul(jnp.concatenate(modes, axis=0), twin[...]) * inv[...]
        wide = lanes_of(values, hb)
        low = thrice(near_low[pl.ds(idx[1], 8), :], wide)
        high = thrice(near_high[pl.ds(idx[1], 8), :], wide)
        lines = []
        for a in range(nx):
            tile = slice(a * NZ, (a + 1) * NZ)
            lines.append(low[:, tile] + turn(high[:, tile], 64))
        columns = []
        for i in range(nx):
            acc = lines[0] * float(t.hart_x[i, 0])
            for a in range(1, nx):
                acc = acc + lines[a] * float(t.hart_x[i, a])
            columns.append(acc)
        out[...] = rmul(jnp.concatenate(columns, axis=0), czh[...])

    def applied(field, al, wxy, ar):
        side = rows_of(lmul(al, lanes_of(field)))
        return rmul(jnp.concatenate([side, field * tiled(wxy, nx)], axis=1), ar)

    def restricted(field, back, hzc):
        columns = []
        for i in range(nx):
            acc = None
            for x in range(8):
                here = field[i * 64 + x * 8 : i * 64 + x * 8 + 8] * float(t.hx[0, x])
                k = (i - 1) % nx
                there = field[k * 64 + x * 8 : k * 64 + x * 8 + 8] * float(t.hx[1, x])
                acc = here + there if acc is None else acc + here + there
            columns.append(acc)
        return rmul(lmul(back, jnp.concatenate(columns, axis=0)), hzc)

    def stage_apply(
        idx, s, below, above, vert, r0, hy, al, tab, ar, back, hzc, z0, q, q0, q7, cq, sums
    ):
        z0[...] = s[...]
        add_faces(is_odd(idx[1]), z0, below, above)
        slabs = []
        for i in range(nx):
            slabs.append(
                hy[0:8] * vert[i * 8 + 1 : i * 8 + 2] + hy[8:16] * vert[i * 8 + 2 : i * 8 + 3]
            )
        pieces = []
        for i in range(nx):
            for x in range(8):
                pieces.append(
                    slabs[i] * float(t.hx[0, x]) + slabs[(i + 1) % nx] * float(t.hx[1, x])
                )
        field = z0[...] + jnp.concatenate(pieces, axis=0)
        z0[...] = field
        wxy, inv_m, inv_mz = tab[0:64], tab[64:128], tab[128:192]
        image = applied(field, al[...], wxy, ar[...])
        sums[0:8] = fold(r0[...] * field * tiled(inv_m, nx))
        sums[8:16] = fold(field * image * tiled(inv_mz, nx))
        cq[...] = restricted(image, back[...], hzc[...])
        q[...] = join_x(image, nx)
        swap_faces(is_odd(idx[1]), q, q0, q7)

    def stage_again(idx, q, below, above, tab, etl, etr, sc, er, el, s, s0, s7, sums, scr):
        scr[...] = q[...]
        add_faces(is_odd(idx[1]), scr, below, above)
        field = scr[...]
        local = smoothed(field, etl[...], etr[...], sc[...], er[...], el[...])
        sums[...] = fold(field * local * tiled(tab[...], nx))
        s[...] = join_x(local, nx)
        swap_faces(is_odd(idx[1]), s, s0, s7)

    def stage_gather(
        idx, s, below, above, z0, cq, sums1, sums2, al, tab, ar, back, hzc, edge, sq, msg, g0, g7
    ):
        sq[...] = s[...]
        add_faces(is_odd(idx[1]), sq, below, above)
        field = sq[...]
        wxy, inv_mz = tab[0:64], tab[128:192]
        image = applied(field, al[...], wxy, ar[...])
        last = total(fold(field * image * tiled(inv_mz, nx)))
        tq = restricted(image, back[...], hzc[...])
        block = cq[0:16] + turn(cq[16:32], 32) + turn(tq[0:16], 64) + turn(tq[16:32], 96)
        lane = lane_index(16)
        row = lax.broadcasted_iota(jnp.int32, (16, NZ), 0)
        values = [total(sums1[0:8]), total(sums1[8:16]), total(sums2[...]), last]
        for k, value in enumerate(values):
            block = block + jnp.where((row == 12) & (lane == NV + k), value, 0.0)
        for k in range(ny):
            msg[k * 16 : k * 16 + 16] = block
        base = pl.multiple_of(idx[0] * 64, 64)
        pair = jnp.concatenate([z0[pl.ds(base, 64), :], sq[pl.ds(base, 64), :]], axis=1)
        slopes = lmul(edge[...], pair)
        start = jnp.concatenate([slopes[0:8, 0:NZ], slopes[0:8, NZ:]], axis=0)
        end = jnp.concatenate([slopes[8:16, 0:NZ], slopes[8:16, NZ:]], axis=0)
        swap_out(is_odd(idx[1]), start, end, g0, g7)

    def stage_final(
        idx,
        reach,
        rec,
        below,
        above,
        z0,
        sq,
        prov,
        g0,
        old,
        hart,
        ez_row,
        around,
        czh,
        gal,
        mky,
        hy,
        left,
        right,
        inv_mz,
        new,
        press,
        scr,
    ):
        cells = jnp.concatenate([rec[pl.ds(a, ny, stride=16), :] for a in range(nx)], axis=1)
        both = lmul(hart[...], cells)
        my, ky = mky[0:ny], mky[ny : 2 * ny]
        lane = lane_index(ny)
        found = []
        levels = 2.0 * (2.0 * ky + ez_row[0:1]) + coarse_shift
        cross = jnp.zeros((ny, NZ), jnp.float32)
        plain = jnp.zeros((ny, NZ), jnp.float32)
        for a in range(nx):
            tile = slice(a * NZ, (a + 1) * NZ)
            comb = both[0:ny, tile] + turn(both[ny : 2 * ny, tile], -32)
            e = jnp.where(lane < NV, comb / (levels + 2.0 * float(t.ex[a])), 0.0)
            found.append(e)
            plain = plain + e * comb
            cross = cross + e * turn(comb, -64)
        grown = rmul(jnp.concatenate(found, axis=0), gal[...])
        quad = jnp.zeros((ny, NZ), jnp.float32)
        for a in range(nx):
            rows = slice(a * ny, (a + 1) * ny)
            mxa, kxa = float(t.mx[a]), float(t.kx[a])
            weight_m = my * (kxa + helmholtz_shift * mxa) + ky * mxa
            weight_k = my * mxa
            quad = quad + found[a] * (
                weight_m * grown[rows, 0:NZ] + weight_k * grown[rows, NZ : 2 * NZ]
            )
        scalars = jnp.sum(rec[pl.ds(12, ny, stride=16), :], axis=0, keepdims=True)
        line = lane_index(1)

        def pick(k):
            return jnp.sum(jnp.where(line == NV + k, scalars, 0.0), axis=1, keepdims=True)

        rz0, zq0 = pick(0), pick(1)
        wq = pick(2) + total(plain)
        ww = pick(3) + 2.0 * total(cross) + total(quad)
        first = rz0 / zq0
        rz1 = rz0 - 2.0 * first * zq0 + first * first * wq
        beta = rz1 / rz0
        grow = 1.0 + beta
        curve = grow * grow * zq0 - 2.0 * grow * first * wq + first * first * ww
        second = rz1 / curve
        on_z = first + second * grow
        on_w = -second * first
        lines = thrice(around[pl.ds(idx[1], 8), :], jnp.concatenate(found, axis=1))
        stack = []
        for xv in range(4):
            base = (idx[0] * 4 + xv) * nx
            acc = lines[:, 0:NZ] * reach[base]
            for a in range(1, nx):
                acc = acc + lines[:, a * NZ : (a + 1) * NZ] * reach[base + a]
            stack.append(acc)
        scr[...] = rmul(jnp.concatenate(stack, axis=0), czh[...]) * on_w
        hy0, hy1 = hy[0:8], hy[8:16]
        slabs = [hy0 * scr[k * 8 + 1 : k * 8 + 2] + hy1 * scr[k * 8 + 2 : k * 8 + 3] for k in range(4)]
        coarse = jnp.concatenate(
            [slabs[1] * float(t.hx[0, x]) + slabs[2] * float(t.hx[1, x]) for x in range(8)], axis=0
        )

        def own(shift):
            base = pl.multiple_of(lax.rem(idx[0] + shift + nx, nx) * 64, 64)
            return z0[pl.ds(base, 64), :] * on_z + sq[pl.ds(base, 64), :] * on_w

        change = own(0) + coarse
        press[...] = old[...] + change
        slopes = lmul(left[...], change)
        gx, gy = slopes[0:64], slopes[64:128]
        gz = rmul(change, right[...])
        prior, later = own(-1), own(1)
        edge0 = 0.5 * (slabs[1] - slabs[0])
        edge7 = 0.5 * (slabs[3] - slabs[2])
        for x in range(8):
            edge0 = edge0 + prior[x * 8 : x * 8 + 8] * float(t.d[7, x])
            edge7 = edge7 + later[x * 8 : x * 8 + 8] * float(t.d[0, x])
        new[0:8] = prov[0:8] - g0[0:8] - 0.5 * (gx[0:8] + edge0)
        new[8:56] = prov[8:56] - g0[8:56] - gx[8:56]
        new[56:64] = prov[56:64] - g0[56:64] - 0.5 * (gx[56:64] + edge7)
        hx0, hx1 = hy0, hy1
        line1 = [scr[k * 8 + 1 : k * 8 + 2] for k in range(4)]
        step0 = [0.5 * (scr[k * 8 + 1 : k * 8 + 2] - scr[k * 8 : k * 8 + 1]) for k in (1, 2)]
        step7 = [0.5 * (scr[k * 8 + 3 : k * 8 + 4] - scr[k * 8 + 2 : k * 8 + 3]) for k in (1, 2)]
        below, above = swap_in(is_odd(idx[1]), below, above)
        under = below[0:8] * on_z + below[8:16] * on_w + hx0 * step0[0] + hx1 * step0[1]
        over = above[0:8] * on_z + above[8:16] * on_w + hx0 * step7[0] + hx1 * step7[1]
        press_y = gy
        new[64:128] = press_y
        own0 = new[pl.ds(64, 8, stride=8), :]
        own7 = new[pl.ds(71, 8, stride=8), :]
        new[pl.ds(64, 8, stride=8), :] = 0.5 * (own0 + under)
        new[pl.ds(71, 8, stride=8), :] = 0.5 * (own7 + over)
        new[64:128] = prov[64:128] - g0[64:128] - new[64:128]
        new[128:192] = prov[128:192] - g0[128:192] - join_z(gz) * inv_mz[...]
        new[192:256] = prov[192:256]

    return (
        stage_state,
        stage_residual,
        stage_smooth,
        stage_coarse,
        stage_apply,
        stage_again,
        stage_gather,
        stage_final,
    )


def exchange(axis, first, second):
    count = lax.axis_size(axis)
    pairs = [(k, k ^ 1) for k in range(count)]
    across = [(k, ((k - 1) ^ 1) + 1) for k in range(1, count - 1)] + [(0, count - 1), (count - 1, 0)]
    return lax.ppermute(first, axis, pairs), lax.ppermute(second, axis, across)


def make_device(t):
    nx, ny, hb = t.nx, t.ny, t.hb
    (
        stage_state,
        stage_residual,
        stage_smooth,
        stage_coarse,
        stage_apply,
        stage_again,
        stage_gather,
        stage_final,
    ) = make_stages(t)
    c = jnp.asarray
    col, ring, face = (64, NZ), (nx * 64, NZ), (nx * 8, NZ)

    def on_device(flow_state, building_height, pressure_old):
        flow = flow_state.reshape(256, NZ)
        old = pressure_old.reshape(64, NZ)
        idx = jnp.stack([lax.axis_index("gx"), lax.axis_index("gy")]).astype(jnp.int32)
        fld, xf0, xf7, kp = call(
            stage_rate,
            [(448, NZ), (56, NZ), (56, NZ), col],
            idx,
            building_height,
            flow,
            old,
            c(t.k1_left),
            c(t.k1_right),
            c(t.visc),
            smem=2,
        )
        below, above = exchange("gx", xf0, xf7)
        fld, yf0, yf7 = call(
            stage_faces, [(448, NZ), (56, NZ), (56, NZ)], idx, fld, below, above, smem=1
        )
        below, above = exchange("gy", yf0, yf7)
        prov, g0, rz, msg = call(
            stage_state,
            [(256, NZ), (192, NZ), col, (ny * 16, NZ)],
            idx,
            fld,
            below,
            above,
            flow,
            kp,
            c(np.concatenate([t.mass, t.inv_bm])),
            c(t.div_left),
            c(t.dz_right),
            c(t.pxy_left),
            c(t.hzm_right),
            smem=1,
            scratch=[pltpu.VMEM((448, NZ), jnp.float32)],
        )
        rec = lax.all_to_all(msg.reshape(ny, 16, NZ), "gy", 0, 0, tiled=True)
        (piece,) = call(
            stage_residual,
            [(64 + hb, NZ)],
            idx,
            rec.reshape(ny * 16, NZ),
            rz,
            c(t.hart_cat),
            smem=1,
        )
        whole = lax.all_gather(piece, "gx", axis=0, tiled=True)
        smoother = (c(t.et_left), c(t.et_right), c(t.scale), c(t.e_right), c(t.e_left))
        r0, s, s0, s7 = call(
            stage_smooth, [ring, ring, face, face], idx, whole, *smoother, smem=1
        )
        below, above = exchange("gy", s0, s7)
        (vert,) = call(
            stage_coarse,
            [face],
            idx,
            whole,
            c(t.coef),
            c(t.twin_right),
            c(t.inv_packed),
            c(t.near_low),
            c(t.near_high),
            c(t.czh_right),
            smem=1,
        )
        tab = c(np.concatenate([t.wxy, t.inv_m, t.inv_mz]))
        operator = (c(t.a_left), tab, c(t.a_right), c(t.back_left), c(t.hzc_right))
        z0, q, q0, q7, cq, sums1 = call(
            stage_apply,
            [ring, ring, face, face, (32, NZ), (16, NZ)],
            idx,
            s,
            below,
            above,
            vert,
            r0,
            c(t.hy),
            *operator,
            smem=1,
        )
        below, above = exchange("gy", q0, q7)
        s, s0, s7, sums2 = call(
            stage_again,
            [ring, face, face, (8, NZ)],
            idx,
            q,
            below,
            above,
            c(t.inv_mz),
            *smoother,
            smem=1,
            scratch=[pltpu.VMEM(ring, jnp.float32)],
        )
        below, above = exchange("gy", s0, s7)
        sq, msg, e0, e7 = call(
            stage_gather,
            [ring, (ny * 16, NZ), (16, NZ), (16, NZ)],
            idx,
            s,
            below,
            above,
            z0,
            cq,
            sums1,
            sums2,
            *operator,
            c(t.edge_left),
            smem=1,
        )
        below, above = exchange("gy", e0, e7)
        rec = lax.all_to_all(msg.reshape(ny, 16, NZ), "gy", 0, 0, tiled=True)
        new, press = call(
            stage_final,
            [(256, NZ), col],
            idx,
            c(t.reach),
            rec.reshape(ny * 16, NZ),
            below,
            above,
            z0,
            sq,
            prov,
            g0,
            old,
            c(t.hart_two),
            c(t.ez_row),
            c(t.near),
            c(t.czh_right),
            c(t.galerkin_right),
            c(t.mky),
            c(t.hy),
            c(t.last_left),
            c(t.dz_right),
            c(t.inv_mz),
            smem=2,
            scratch=[pltpu.VMEM((32, NZ), jnp.float32)],
        )
        return new.reshape(flow_state.shape), press.reshape(pressure_old.shape)

    return on_device


def solution(mesh):
    t = Tables(mesh.shape["gx"], mesh.shape["gy"])
    in_specs = (P(None, "gx", "gy", None), P("gx", "gy"), P("gx", "gy", None))
    out_specs = (P(None, "gx", "gy", None), P("gx", "gy", None))
    return jax.shard_map(
        make_device(t), mesh=mesh, in_specs=in_specs, out_specs=out_specs, check_vma=False
    )
```

```python
import math

import jax
import jax.numpy as jnp
import ml_dtypes
import numpy as np
from jax import lax
from jax.experimental import pallas as pl
from jax.experimental.pallas import tpu as pltpu
from jax.sharding import PartitionSpec as P

INTERPRET = False
VMEM_LIMIT = 16 * 1024 * 1024

viscosity = 0.05
time_step = 0.01
drag_strength = 20.0
heating = 40.0
buoyancy = 10.0
helmholtz_shift = 0.001
local_shift = 0.5
coarse_shift = 0.02
gll_points = (
    -1.0,
    -0.8717401485096066,
    -0.5917001814331423,
    -0.2092992179024789,
    0.2092992179024789,
    0.5917001814331423,
    0.8717401485096066,
    1.0,
)
EZ = 16
NZ = 128
NV = 17


def legendre_seven(points):
    squared = points * points
    return points * (((429.0 * squared - 693.0) * squared + 315.0) * squared - 35.0) / 16.0


def jacobi_eigen(matrix):
    current = np.array(matrix)
    basis = np.eye(8)
    for rounds in range(12):
        for first in range(7):
            for second in range(first + 1, 8):
                angle = 0.5 * math.atan2(
                    2.0 * float(current[first, second]),
                    float(current[second, second] - current[first, first]),
                )
                cosine = math.cos(angle)
                sine = math.sin(angle)
                rotation = np.eye(8)
                rotation[first, first] = cosine
                rotation[second, second] = cosine
                rotation[first, second] = sine
                rotation[second, first] = -sine
                current = rotation.T @ current @ rotation
                basis = basis @ rotation
    return (np.sum(current * np.eye(8), axis=0), basis)


def gll_tables():
    nodes = np.array(gll_points)
    values = legendre_seven(nodes)
    weights = 2.0 / (56.0 * values * values)
    differ = nodes[:, None] - nodes[None, :] + np.eye(8)
    derivative = values[:, None] / values[None, :] / differ * (1.0 - np.eye(8))
    ends = np.array([-14.0, 0.0, 0.0, 0.0, 0.0, 0.0, 0.0, 14.0])
    derivative = derivative + np.eye(8) * ends[None, :]
    stiffness = derivative.T @ (weights[:, None] * derivative)
    scaled = stiffness / np.sqrt(np.outer(weights, weights))
    scaled = 0.5 * (scaled + scaled.T)
    eigen_values, eigen_vectors = jacobi_eigen(scaled)
    eigen_basis = eigen_vectors / np.sqrt(weights)[:, None]
    return (nodes, weights, derivative, eigen_basis, np.maximum(eigen_values, 0.0))


def parts(table):
    table = np.asarray(table, np.float32)
    high = table.astype(ml_dtypes.bfloat16)
    low = (table - high.astype(np.float32)).astype(ml_dtypes.bfloat16)
    return high, low


def parts_three(table):
    high, low = parts(table)
    rest = np.asarray(table, np.float64) - high.astype(np.float64) - low.astype(np.float64)
    return high, low, rest.astype(ml_dtypes.bfloat16)


def left5(table):
    high, low, rest = parts_three(table)
    return np.concatenate([high, high, low, low, rest], axis=1)


def right5(table):
    return np.concatenate(parts_three(table), axis=0)


def left3(table):
    high, low = parts(table)
    return np.concatenate([high, high, low], axis=1)


def right3(table):
    return np.concatenate(parts(table), axis=0)


def split(field):
    high = field.astype(jnp.bfloat16)
    low = (field - high.astype(jnp.float32)).astype(jnp.bfloat16)
    return high, low


def stacked(field, terms, axis):
    high, low = split(field)
    order = [high, low, high, low, high] if terms == 5 else [high, low, high]
    return jnp.concatenate(order, axis=axis)


def lmul(table, field):
    terms = table.shape[1] // field.shape[0]
    return jnp.dot(table, stacked(field, terms, 0), preferred_element_type=jnp.float32)


def rmul(field, table):
    size = field.shape[1]
    part = [table[k : k + size] for k in range(0, table.shape[0], size)]
    order = [part[0], part[0], part[1], part[1], part[2]] if len(part) == 3 else [part[0]] + part
    return jnp.dot(
        stacked(field, len(order), 1),
        jnp.concatenate(order, axis=0),
        preferred_element_type=jnp.float32,
    )


def thrice(table, field):
    high, low = split(table)
    first, second = split(field)
    out = jnp.dot(high, first, preferred_element_type=jnp.float32)
    out = out + jnp.dot(high, second, preferred_element_type=jnp.float32)
    return out + jnp.dot(low, first, preferred_element_type=jnp.float32)


def lanes_of(field, size=64):
    return jnp.concatenate(
        [field[k * size : (k + 1) * size] for k in range(field.shape[0] // size)], axis=1
    )


def rows_of(field):
    return jnp.concatenate(
        [field[:, k * NZ : (k + 1) * NZ] for k in range(field.shape[1] // NZ)], axis=0
    )


def lane_index(rows):
    return lax.broadcasted_iota(jnp.int32, (rows, NZ), 1)


def turn(field, shift):
    return pltpu.roll(field, shift % NZ, 1)


def join_z(field):
    lane = lane_index(field.shape[0])
    ahead = jnp.where((lane % 8 == 7) & (lane < NZ - 1), turn(field, -1), 0.0)
    behind = jnp.where((lane % 8 == 0) & (lane > 0), turn(field, 1), 0.0)
    return field + ahead + behind


def join_x(rows, count):
    blocks = [rows[k * 64 : (k + 1) * 64] for k in range(count)]
    sums = [blocks[k][0:8] + blocks[(k - 1) % count][56:64] for k in range(count)]
    pieces = []
    for k in range(count):
        pieces += [sums[k], blocks[k][8:56], sums[(k + 1) % count]]
    return jnp.concatenate(pieces, axis=0)


def fold(field):
    return jnp.sum(field.reshape(field.shape[0] // 8, 8, NZ), axis=0)


def total(field):
    return jnp.sum(jnp.sum(field, axis=0, keepdims=True), axis=1, keepdims=True)


def tiled(table, count):
    return jnp.concatenate([table] * count, axis=0)


class Tables:
    def __init__(self, nx, ny):
        nodes, w, d, e, lam = gll_tables()
        self.nx, self.ny = nx, ny
        eye8 = np.eye(8)
        kx = d.T @ (w[:, None] * d)
        bx = np.diag(w)
        eyez = np.eye(EZ)
        join = np.eye(NZ)
        for k in range(EZ - 1):
            join[8 * k + 7, 8 * k + 8] = 1.0
            join[8 * k + 8, 8 * k + 7] = 1.0
        dz_t = np.kron(eyez, d).T
        kz_t = np.kron(eyez, kx).T
        wz = np.tile(w, EZ)
        wxy = np.kron(w, w)
        mz = join.sum(axis=1)
        m1 = np.array([2.0, 1, 1, 1, 1, 1, 1, 2.0])
        mxy = np.kron(m1, m1)
        f32 = np.float32
        mass = np.outer(wxy, wz)
        self.mass = mass.astype(f32)
        self.wz = np.broadcast_to(wz[None, :], (64, NZ)).astype(f32)
        self.wxy = np.broadcast_to(wxy[:, None], (64, NZ)).astype(f32)
        self.inv_bm = (1.0 / (mass * np.outer(mxy, mz))).astype(f32)
        self.inv_m = (1.0 / np.outer(mxy, mz)).astype(f32)
        self.inv_mz = np.broadcast_to(1.0 / mz[None, :], (64, NZ)).astype(f32)
        self.visc = np.stack([self.mass, self.wz, self.wxy]).reshape(192, NZ)
        dx = np.kron(d, eye8)
        dy = np.kron(eye8, d)
        lv = np.kron(kx, bx) + np.kron(bx, kx)
        self.k1_left = left5(np.concatenate([dx, dy, lv], axis=0))
        self.k1_right = right5(np.concatenate([dz_t, kz_t], axis=1))
        self.div_left = left5(np.concatenate([dx, dy], axis=1))
        self.dz_right = right5(dz_t)
        hx = np.stack([(1.0 - nodes) / 2.0, (1.0 + nodes) / 2.0])
        self.hx = hx
        hz = np.zeros((NZ, NV))
        for z in range(NZ):
            hz[z, z // 8] = hx[0, z % 8]
            hz[z, z // 8 + 1] = hx[1, z % 8]
        pxy = np.zeros((8, 64))
        for xv in range(2):
            for yv in range(2):
                pxy[xv * 2 + yv] = np.kron(hx[xv], hx[yv])
        self.pxy_left = left3(pxy)
        hzm = np.zeros((NZ, NZ))
        hzm[:, :NV] = hz / mz[:, None]
        self.hzm_right = right3(hzm)
        self.hy = np.broadcast_to(hx.reshape(16, 1), (16, NZ)).astype(f32)

        def hartley(count):
            angle = 2.0 * np.pi / count * np.outer(np.arange(count), np.arange(count))
            return (np.cos(angle) + np.sin(angle)) / np.sqrt(count)

        self.hart_x = hartley(nx)
        hart_y = hartley(ny)
        ex = 2.0 - 2.0 * np.cos(2.0 * np.pi / nx * np.arange(nx))
        ey = 2.0 - 2.0 * np.cos(2.0 * np.pi / ny * np.arange(ny))
        ez = 2.0 - 2.0 * np.cos(np.pi / NV * np.arange(NV))
        levels = np.arange(NV)
        norms = np.where(levels == 0, np.sqrt(1.0 / NV), np.sqrt(2.0 / NV))
        cz = np.cos(np.pi / NV * np.outer(levels + 0.5, levels)) * norms[None, :]
        inverse = 1.0 / (
            2.0 * (ex[:, None, None] + ey[None, :, None] + ez[None, None, :]) + coarse_shift
        )
        shifted = np.roll(hart_y, -1, axis=1)
        self.hart_two = left3(np.concatenate([hart_y, shifted], axis=0))
        toward = np.zeros((32, nx * 8))
        for yv in range(2):
            for xv in range(2):
                for i in range(nx):
                    toward[yv * 16 : yv * 16 + nx, i * 8 + xv * 2 + yv] = self.hart_x[
                        :, (i + xv) % nx
                    ]
        self.toward_left = left3(toward)
        levels_only = np.zeros((NZ, NZ))
        levels_only[:NV, :NV] = cz
        self.levels_right = right3(levels_only)
        near = hart_y[(np.arange(ny + 8) - 1) % ny]
        self.near = near.astype(f32)
        czh = np.zeros((NZ, NZ))
        czh[:NV] = (hz @ cz).T
        self.czh_right = right3(czh)
        self.et_left = left3(np.kron(e.T, e.T))
        self.e_left = left3(np.kron(e, e))
        self.et_right = right3(np.kron(eyez, e))
        self.e_right = right3(np.kron(eyez, e.T) @ join)
        lxy = (lam[:, None] + lam[None, :]).reshape(64)
        self.scale = (1.0 / (lxy[:, None] + np.tile(lam, EZ)[None, :] + local_shift)).astype(f32)
        self.a_left = left5(lv + helmholtz_shift * np.kron(bx, bx))
        self.a_right = right5(np.concatenate([wz[:, None] * join, kz_t @ join], axis=0))
        back = np.zeros((32, nx * 8))
        for yv in range(2):
            for a in range(nx):
                for i in range(nx):
                    back[yv * 16 + a, i * 8 : i * 8 + 8] = self.hart_x[a, i] * hx[yv]
        self.back_left = left3(back)
        hzc = np.zeros((NZ, NZ))
        hzc[:, :NV] = (hz / mz[:, None]) @ cz
        self.hzc_right = right3(hzc)
        self.edge_left = left3(np.concatenate([np.kron(eye8, d[:1]), np.kron(eye8, d[7:])], axis=0))
        self.ex = ex
        ez_row = np.zeros((8, NZ))
        ez_row[:, :NV] = ez
        self.ez_row = ez_row.astype(f32)
        reach = np.zeros((nx, 4, nx))
        for i in range(nx):
            for xv in range(4):
                reach[i, xv] = self.hart_x[(i + xv - 1) % nx]
        self.reach = reach.reshape(-1).astype(f32)
        second = np.diag(2.0 * np.ones(NV)) - np.eye(NV, k=1) - np.eye(NV, k=-1)
        second[0, 0] = second[-1, -1] = 1.0
        double = 2.0 * np.ones(NV)
        double[0] = double[-1] = 1.0
        mass_z = np.diag(double) - second / 3.0
        both = np.zeros((NZ, 2 * NZ))
        both[:NV, :NV] = cz.T @ mass_z @ cz
        both[:NV, NZ : NZ + NV] = cz.T @ (second / 2.0) @ cz
        self.galerkin_right = right3(both)
        self.mx = 2.0 - ex / 3.0
        self.kx = ex / 2.0
        my = np.broadcast_to((2.0 - ey / 3.0)[:, None], (ny, NZ))
        ky = np.broadcast_to((ey / 2.0)[:, None], (ny, NZ))
        self.mky = np.concatenate([my, ky], axis=0).astype(f32)
        self.last_left = left5(np.concatenate([dx, dy], axis=0))
        self.d = d


def call(kernel, outs, *args, scratch=(), smem=0, space=pltpu.VMEM, limit=VMEM_LIMIT):
    specs = [pl.BlockSpec(memory_space=pltpu.SMEM)] * smem
    specs += [pl.BlockSpec(memory_space=space)] * (len(args) - smem)
    return pl.pallas_call(
        kernel,
        out_shape=[jax.ShapeDtypeStruct(shape, jnp.float32) for shape in outs],
        in_specs=specs,
        out_specs=[pl.BlockSpec(memory_space=pltpu.VMEM)] * len(outs),
        scratch_shapes=list(scratch),
        interpret=INTERPRET,
        compiler_params=pltpu.CompilerParams(vmem_limit_bytes=limit),
        name=kernel.__name__,
    )(*args)


def stage_rate(idx, h, *refs):
    sources, (fld, xa, xb, kp), landed, sems = refs[:5], refs[5:9], refs[9:14], refs[14]
    copies = [
        pltpu.make_async_copy(source, place, sems.at[k])
        for k, (source, place) in enumerate(zip(sources, landed))
    ]
    for copy in copies:
        copy.start()
    for copy in copies:
        copy.wait()
    flow, old, left, right, tab = landed
    f = [flow[q * 64 : q * 64 + 64] for q in range(4)]
    p = old[...]
    lx = lmul(left[...], jnp.concatenate(f + [p], axis=1))
    rx = rmul(jnp.concatenate(f + [p], axis=0), right[...])
    mass, wz, wxy = tab[0:64], tab[64:128], tab[128:192]
    u, v, w, theta = f
    drag = drag_strength * jnp.sqrt(u * u + v * v + w * w)
    canopy = (lane_index(64) // 8 < h[0, 0]).astype(jnp.float32)
    drag = drag * canopy
    forcing = [-drag * u, -drag * v, -drag * w + buoyancy * theta, heating * canopy]
    for q in range(5):
        lane = slice(q * NZ, q * NZ + NZ)
        rows = slice(q * 64, q * 64 + 64)
        gx, gy, lv = lx[0:64, lane], lx[64:128, lane], lx[128:192, lane]
        gz, kz = rx[rows, 0:NZ], rx[rows, NZ : 2 * NZ]
        stiff = lv * wz + wxy * kz
        if q < 4:
            rate = mass * (forcing[q] - (u * gx + v * gy + w * gz)) - viscosity * stiff
            fld[rows] = join_z(rate)
        else:
            kp[...] = stiff + helmholtz_shift * mass * p
            for k, grad in enumerate((gx, gy, gz)):
                fld[(4 + k) * 64 : (5 + k) * 64] = join_z(mass * grad)
    start = jnp.concatenate([fld[q * 64 : q * 64 + 8] for q in range(7)], axis=0)
    end = jnp.concatenate([fld[q * 64 + 56 : q * 64 + 64] for q in range(7)], axis=0)
    swap_out(is_odd(idx[0]), start, end, xa, xb)


def stage_faces(idx, fld, xa, xb, out, ya, yb):
    below, above = swap_in(is_odd(idx[0]), xa, xb)
    for q in range(7):
        base = q * 64
        out[base : base + 8] = fld[base : base + 8] + below[q * 8 : q * 8 + 8]
        out[base + 8 : base + 56] = fld[base + 8 : base + 56]
        out[base + 56 : base + 64] = fld[base + 56 : base + 64] + above[q * 8 : q * 8 + 8]
    swap_faces(is_odd(idx[1]), out, ya, yb)


def swap_faces(odd, ref, first, second):
    count = ref.shape[0] // 8
    start = ref[pl.ds(0, count, stride=8), :]
    end = ref[pl.ds(7, count, stride=8), :]
    swap_out(odd, start, end, first, second)


def add_faces(odd, ref, first, second):
    below, above = swap_in(odd, first, second)
    count = ref.shape[0] // 8
    ref[pl.ds(0, count, stride=8), :] = ref[pl.ds(0, count, stride=8), :] + below
    ref[pl.ds(7, count, stride=8), :] = ref[pl.ds(7, count, stride=8), :] + above


def swap_out(odd, start, end, first, second):
    first[...] = jnp.where(odd, start, end)
    second[...] = jnp.where(odd, end, start)


def swap_in(odd, first, second):
    return jnp.where(odd, first[...], second[...]), jnp.where(odd, second[...], first[...])


def is_odd(index):
    return lax.rem(index, 2) == 1


def make_stages(t):
    nx, ny = t.nx, t.ny

    def stage_state(
        idx, fx, below, above, flow, kp, tab, dleft, dright, pleft, hright, prov, g0, piece, scr
    ):
        scr[...] = fx[...]
        add_faces(is_odd(idx[1]), scr, below, above)
        mass, inv_bm = tab[0:64], tab[64:128]
        lane = lane_index(64)
        new = []
        for q in range(4):
            rows = slice(q * 64, q * 64 + 64)
            value = flow[rows] + time_step * scr[rows] * inv_bm
            if q == 2:
                value = jnp.where((lane == 0) | (lane == NZ - 1), 0.0, value)
            prov[rows] = value
            new.append(value)
        for k in range(3):
            g0[k * 64 : k * 64 + 64] = scr[(4 + k) * 64 : (5 + k) * 64] * inv_bm
        div = lmul(dleft[...], jnp.concatenate(new[:2], axis=0)) + rmul(new[2], dright[...])
        joined = join_z(-mass * div - kp[...])
        piece[0:64] = joined
        piece[64:72] = rmul(lmul(pleft[...], joined), hright[...])

    def send(msg, block):
        for k in range(ny):
            msg[k * 16 : k * 16 + 16] = block

    def stage_ring(idx, ring, toward, levels, r, ra, rb, msg):
        rows = jnp.concatenate([ring[i * 72 : i * 72 + 64] for i in range(nx)], axis=0)
        r[...] = join_x(rows, nx)
        swap_faces(is_odd(idx[1]), r, ra, rb)
        corners = jnp.concatenate([ring[i * 72 + 64 : i * 72 + 72] for i in range(nx)], axis=0)
        modes = rmul(lmul(toward[...], corners), levels[...])
        send(msg, modes[0:16] + turn(modes[16:32], 32))

    def smoothed(field, etl, etr, sc, er, el):
        modal = rmul(rows_of(lmul(etl, lanes_of(field))), etr)
        modal = rmul(modal * tiled(sc, nx), er)
        return rows_of(lmul(el, lanes_of(modal)))

    def stage_smooth(idx, r, ra, rb, etl, etr, sc, er, el, r0, s, s0, s7):
        r0[...] = r[...]
        add_faces(is_odd(idx[1]), r0, ra, rb)
        local = smoothed(r0[...], etl[...], etr[...], sc[...], er[...], el[...])
        s[...] = join_x(local, nx)
        swap_faces(is_odd(idx[1]), s, s0, s7)

    def spectra(rec, hart, ez_row, ky):
        cells = jnp.concatenate([rec[pl.ds(a, ny, stride=16), :] for a in range(nx)], axis=1)
        both = lmul(hart, cells)
        lane = lane_index(ny)
        levels = 2.0 * (2.0 * ky + ez_row) + coarse_shift
        found = []
        for a in range(nx):
            tile = slice(a * NZ, (a + 1) * NZ)
            comb = both[0:ny, tile] + turn(both[ny : 2 * ny, tile], -32)
            e = jnp.where(lane < NV, comb / (levels + 2.0 * float(t.ex[a])), 0.0)
            found.append((comb, e))
        return found

    def stage_coarse(idx, rec, hart, ez_row, mky, around, czh, out):
        found = spectra(rec, hart[...], ez_row[0:1], mky[ny : 2 * ny])
        wide = jnp.concatenate([e for _, e in found], axis=1)
        lines = thrice(around[pl.ds(idx[1], 8), :], wide)
        columns = []
        for i in range(nx):
            acc = lines[:, 0:NZ] * float(t.hart_x[i, 0])
            for a in range(1, nx):
                acc = acc + lines[:, a * NZ : (a + 1) * NZ] * float(t.hart_x[i, a])
            columns.append(acc)
        out[...] = rmul(jnp.concatenate(columns, axis=0), czh[...])

    def applied(field, al, wxy, ar):
        side = rows_of(lmul(al, lanes_of(field)))
        return rmul(jnp.concatenate([side, field * tiled(wxy, nx)], axis=1), ar)

    def restricted(field, back, hzc):
        columns = []
        for i in range(nx):
            acc = None
            for x in range(8):
                here = field[i * 64 + x * 8 : i * 64 + x * 8 + 8] * float(t.hx[0, x])
                k = (i - 1) % nx
                there = field[k * 64 + x * 8 : k * 64 + x * 8 + 8] * float(t.hx[1, x])
                acc = here + there if acc is None else acc + here + there
            columns.append(acc)
        return rmul(lmul(back, jnp.concatenate(columns, axis=0)), hzc)

    def stage_apply(
        idx, s, below, above, vert, r0, hy, al, tab, ar, back, hzc, z0, q, q0, q7, cq, sums
    ):
        z0[...] = s[...]
        add_faces(is_odd(idx[1]), z0, below, above)
        slabs = []
        for i in range(nx):
            slabs.append(
                hy[0:8] * vert[i * 8 + 1 : i * 8 + 2] + hy[8:16] * vert[i * 8 + 2 : i * 8 + 3]
            )
        pieces = []
        for i in range(nx):
            for x in range(8):
                pieces.append(
                    slabs[i] * float(t.hx[0, x]) + slabs[(i + 1) % nx] * float(t.hx[1, x])
                )
        field = z0[...] + jnp.concatenate(pieces, axis=0)
        z0[...] = field
        wxy, inv_m, inv_mz = tab[0:64], tab[64:128], tab[128:192]
        image = applied(field, al[...], wxy, ar[...])
        sums[0:8] = fold(r0[...] * field * tiled(inv_m, nx))
        sums[8:16] = fold(field * image * tiled(inv_mz, nx))
        cq[...] = restricted(image, back[...], hzc[...])
        q[...] = join_x(image, nx)
        swap_faces(is_odd(idx[1]), q, q0, q7)

    def stage_again(idx, q, below, above, tab, etl, etr, sc, er, el, s, s0, s7, sums, scr):
        scr[...] = q[...]
        add_faces(is_odd(idx[1]), scr, below, above)
        field = scr[...]
        local = smoothed(field, etl[...], etr[...], sc[...], er[...], el[...])
        sums[...] = fold(field * local * tiled(tab[...], nx))
        s[...] = join_x(local, nx)
        swap_faces(is_odd(idx[1]), s, s0, s7)

    def stage_gather(
        idx, s, below, above, z0, cq, sums1, sums2, al, tab, ar, back, hzc, edge, sq, msg, g0, g7
    ):
        sq[...] = s[...]
        add_faces(is_odd(idx[1]), sq, below, above)
        field = sq[...]
        wxy, inv_mz = tab[0:64], tab[128:192]
        image = applied(field, al[...], wxy, ar[...])
        last = total(fold(field * image * tiled(inv_mz, nx)))
        tq = restricted(image, back[...], hzc[...])
        block = cq[0:16] + turn(cq[16:32], 32) + turn(tq[0:16], 64) + turn(tq[16:32], 96)
        lane = lane_index(16)
        row = lax.broadcasted_iota(jnp.int32, (16, NZ), 0)
        values = [total(sums1[0:8]), total(sums1[8:16]), total(sums2[...]), last]
        for k, value in enumerate(values):
            block = block + jnp.where((row == 12) & (lane == NV + k), value, 0.0)
        send(msg, block)
        base = pl.multiple_of(idx[0] * 64, 64)
        pair = jnp.concatenate([z0[pl.ds(base, 64), :], sq[pl.ds(base, 64), :]], axis=1)
        slopes = lmul(edge[...], pair)
        start = jnp.concatenate([slopes[0:8, 0:NZ], slopes[0:8, NZ:]], axis=0)
        end = jnp.concatenate([slopes[8:16, 0:NZ], slopes[8:16, NZ:]], axis=0)
        swap_out(is_odd(idx[1]), start, end, g0, g7)

    def stage_final(
        idx,
        reach,
        rec,
        below,
        above,
        z0,
        sq,
        prov,
        g0,
        old,
        hart,
        ez_row,
        around,
        czh,
        gal,
        mky,
        hy,
        left,
        right,
        inv_mz,
        new,
        press,
        scr,
    ):
        my, ky = mky[0:ny], mky[ny : 2 * ny]
        cross = jnp.zeros((ny, NZ), jnp.float32)
        plain = jnp.zeros((ny, NZ), jnp.float32)
        found = []
        for comb, e in spectra(rec, hart[...], ez_row[0:1], ky):
            found.append(e)
            plain = plain + e * comb
            cross = cross + e * turn(comb, -64)
        grown = rmul(jnp.concatenate(found, axis=0), gal[...])
        quad = jnp.zeros((ny, NZ), jnp.float32)
        for a in range(nx):
            rows = slice(a * ny, (a + 1) * ny)
            mxa, kxa = float(t.mx[a]), float(t.kx[a])
            weight_m = my * (kxa + helmholtz_shift * mxa) + ky * mxa
            weight_k = my * mxa
            quad = quad + found[a] * (
                weight_m * grown[rows, 0:NZ] + weight_k * grown[rows, NZ : 2 * NZ]
            )
        scalars = jnp.sum(rec[pl.ds(12, ny, stride=16), :], axis=0, keepdims=True)
        line = lane_index(1)

        def pick(k):
            return jnp.sum(jnp.where(line == NV + k, scalars, 0.0), axis=1, keepdims=True)

        rz0, zq0 = pick(0), pick(1)
        wq = pick(2) + total(plain)
        ww = pick(3) + 2.0 * total(cross) + total(quad)
        first = rz0 / zq0
        rz1 = rz0 - 2.0 * first * zq0 + first * first * wq
        beta = rz1 / rz0
        grow = 1.0 + beta
        curve = grow * grow * zq0 - 2.0 * grow * first * wq + first * first * ww
        second = rz1 / curve
        on_z = first + second * grow
        on_w = -second * first
        lines = thrice(around[pl.ds(idx[1], 8), :], jnp.concatenate(found, axis=1))
        stack = []
        for xv in range(4):
            base = (idx[0] * 4 + xv) * nx
            acc = lines[:, 0:NZ] * reach[base]
            for a in range(1, nx):
                acc = acc + lines[:, a * NZ : (a + 1) * NZ] * reach[base + a]
            stack.append(acc)
        scr[...] = rmul(jnp.concatenate(stack, axis=0), czh[...]) * on_w
        hy0, hy1 = hy[0:8], hy[8:16]
        slabs = [hy0 * scr[k * 8 + 1 : k * 8 + 2] + hy1 * scr[k * 8 + 2 : k * 8 + 3] for k in range(4)]
        coarse = jnp.concatenate(
            [slabs[1] * float(t.hx[0, x]) + slabs[2] * float(t.hx[1, x]) for x in range(8)], axis=0
        )

        def own(shift):
            base = pl.multiple_of(lax.rem(idx[0] + shift + nx, nx) * 64, 64)
            return z0[pl.ds(base, 64), :] * on_z + sq[pl.ds(base, 64), :] * on_w

        change = own(0) + coarse
        press[...] = old[...] + change
        slopes = lmul(left[...], change)
        gx, gy = slopes[0:64], slopes[64:128]
        gz = rmul(change, right[...])
        prior, later = own(-1), own(1)
        edge0 = 0.5 * (slabs[1] - slabs[0])
        edge7 = 0.5 * (slabs[3] - slabs[2])
        for x in range(8):
            edge0 = edge0 + prior[x * 8 : x * 8 + 8] * float(t.d[7, x])
            edge7 = edge7 + later[x * 8 : x * 8 + 8] * float(t.d[0, x])
        new[0:8] = prov[0:8] - g0[0:8] - 0.5 * (gx[0:8] + edge0)
        new[8:56] = prov[8:56] - g0[8:56] - gx[8:56]
        new[56:64] = prov[56:64] - g0[56:64] - 0.5 * (gx[56:64] + edge7)
        hx0, hx1 = hy0, hy1
        line1 = [scr[k * 8 + 1 : k * 8 + 2] for k in range(4)]
        step0 = [0.5 * (scr[k * 8 + 1 : k * 8 + 2] - scr[k * 8 : k * 8 + 1]) for k in (1, 2)]
        step7 = [0.5 * (scr[k * 8 + 3 : k * 8 + 4] - scr[k * 8 + 2 : k * 8 + 3]) for k in (1, 2)]
        below, above = swap_in(is_odd(idx[1]), below, above)
        under = below[0:8] * on_z + below[8:16] * on_w + hx0 * step0[0] + hx1 * step0[1]
        over = above[0:8] * on_z + above[8:16] * on_w + hx0 * step7[0] + hx1 * step7[1]
        press_y = gy
        new[64:128] = press_y
        own0 = new[pl.ds(64, 8, stride=8), :]
        own7 = new[pl.ds(71, 8, stride=8), :]
        new[pl.ds(64, 8, stride=8), :] = 0.5 * (own0 + under)
        new[pl.ds(71, 8, stride=8), :] = 0.5 * (own7 + over)
        new[64:128] = prov[64:128] - g0[64:128] - new[64:128]
        new[128:192] = prov[128:192] - g0[128:192] - join_z(gz) * inv_mz[...]
        new[192:256] = prov[192:256]

    return (
        stage_state,
        stage_ring,
        stage_smooth,
        stage_coarse,
        stage_apply,
        stage_again,
        stage_gather,
        stage_final,
    )


def exchange(axis, first, second):
    count = lax.axis_size(axis)
    pairs = [(k, k ^ 1) for k in range(count)]
    across = [(k, ((k - 1) ^ 1) + 1) for k in range(1, count - 1)] + [(0, count - 1), (count - 1, 0)]
    return lax.ppermute(first, axis, pairs), lax.ppermute(second, axis, across)


def make_device(t):
    nx, ny = t.nx, t.ny
    (
        stage_state,
        stage_ring,
        stage_smooth,
        stage_coarse,
        stage_apply,
        stage_again,
        stage_gather,
        stage_final,
    ) = make_stages(t)
    c = jnp.asarray
    col, ring, face = (64, NZ), (nx * 64, NZ), (nx * 8, NZ)

    def on_device(flow_state, building_height, pressure_old):
        flow = flow_state.reshape(256, NZ)
        old = pressure_old.reshape(64, NZ)
        idx = jnp.stack([lax.axis_index("gx"), lax.axis_index("gy")]).astype(jnp.int32)
        fld, xf0, xf7, kp = call(
            stage_rate,
            [(448, NZ), (56, NZ), (56, NZ), col],
            idx,
            building_height,
            flow,
            old,
            c(t.k1_left),
            c(t.k1_right),
            c(t.visc),
            smem=2,
            space=pltpu.HBM,
            limit=60 * 1024 * 1024,
            scratch=[
                pltpu.VMEM((256, NZ), jnp.float32),
                pltpu.VMEM((64, NZ), jnp.float32),
                pltpu.VMEM(t.k1_left.shape, jnp.bfloat16),
                pltpu.VMEM(t.k1_right.shape, jnp.bfloat16),
                pltpu.VMEM(t.visc.shape, jnp.float32),
                pltpu.SemaphoreType.DMA((5,)),
            ],
        )
        below, above = exchange("gx", xf0, xf7)
        fld, yf0, yf7 = call(
            stage_faces, [(448, NZ), (56, NZ), (56, NZ)], idx, fld, below, above, smem=1
        )
        below, above = exchange("gy", yf0, yf7)
        prov, g0, piece = call(
            stage_state,
            [(256, NZ), (192, NZ), (72, NZ)],
            idx,
            fld,
            below,
            above,
            flow,
            kp,
            c(np.concatenate([t.mass, t.inv_bm])),
            c(t.div_left),
            c(t.dz_right),
            c(t.pxy_left),
            c(t.hzm_right),
            smem=1,
            scratch=[pltpu.VMEM((448, NZ), jnp.float32)],
        )
        whole = lax.all_gather(piece, "gx", axis=0, tiled=True)
        r, ra, rb, msg = call(
            stage_ring,
            [ring, face, face, (ny * 16, NZ)],
            idx,
            whole,
            c(t.toward_left),
            c(t.levels_right),
            smem=1,
        )
        rec = lax.all_to_all(msg.reshape(ny, 16, NZ), "gy", 0, 0, tiled=True)
        below, above = exchange("gy", ra, rb)
        smoother = (c(t.et_left), c(t.et_right), c(t.scale), c(t.e_right), c(t.e_left))
        r0, s, s0, s7 = call(
            stage_smooth, [ring, ring, face, face], idx, r, below, above, *smoother, smem=1
        )
        below, above = exchange("gy", s0, s7)
        (vert,) = call(
            stage_coarse,
            [face],
            idx,
            rec.reshape(ny * 16, NZ),
            c(t.hart_two),
            c(t.ez_row),
            c(t.mky),
            c(t.near),
            c(t.czh_right),
            smem=1,
        )
        tab = c(np.concatenate([t.wxy, t.inv_m, t.inv_mz]))
        operator = (c(t.a_left), tab, c(t.a_right), c(t.back_left), c(t.hzc_right))
        z0, q, q0, q7, cq, sums1 = call(
            stage_apply,
            [ring, ring, face, face, (32, NZ), (16, NZ)],
            idx,
            s,
            below,
            above,
            vert,
            r0,
            c(t.hy),
            *operator,
            smem=1,
        )
        below, above = exchange("gy", q0, q7)
        s, s0, s7, sums2 = call(
            stage_again,
            [ring, face, face, (8, NZ)],
            idx,
            q,
            below,
            above,
            c(t.inv_mz),
            *smoother,
            smem=1,
            scratch=[pltpu.VMEM(ring, jnp.float32)],
        )
        below, above = exchange("gy", s0, s7)
        sq, msg, e0, e7 = call(
            stage_gather,
            [ring, (ny * 16, NZ), (16, NZ), (16, NZ)],
            idx,
            s,
            below,
            above,
            z0,
            cq,
            sums1,
            sums2,
            *operator,
            c(t.edge_left),
            smem=1,
        )
        below, above = exchange("gy", e0, e7)
        rec = lax.all_to_all(msg.reshape(ny, 16, NZ), "gy", 0, 0, tiled=True)
        new, press = call(
            stage_final,
            [(256, NZ), col],
            idx,
            c(t.reach),
            rec.reshape(ny * 16, NZ),
            below,
            above,
            z0,
            sq,
            prov,
            g0,
            old,
            c(t.hart_two),
            c(t.ez_row),
            c(t.near),
            c(t.czh_right),
            c(t.galerkin_right),
            c(t.mky),
            c(t.hy),
            c(t.last_left),
            c(t.dz_right),
            c(t.inv_mz),
            smem=2,
            scratch=[pltpu.VMEM((32, NZ), jnp.float32)],
        )
        return new.reshape(flow_state.shape), press.reshape(pressure_old.shape)

    return on_device


def solution(mesh):
    t = Tables(mesh.shape["gx"], mesh.shape["gy"])
    in_specs = (P(None, "gx", "gy", None), P("gx", "gy"), P("gx", "gy", None))
    out_specs = (P(None, "gx", "gy", None), P("gx", "gy", None))
    return jax.shard_map(
        make_device(t), mesh=mesh, in_specs=in_specs, out_specs=out_specs, check_vma=False
    )
```

```python
import math

import jax
import jax.numpy as jnp
import ml_dtypes
import numpy as np
from jax import lax
from jax.experimental import pallas as pl
from jax.experimental.pallas import tpu as pltpu
from jax.sharding import PartitionSpec as P

INTERPRET = False
VMEM_LIMIT = 16 * 1024 * 1024

viscosity = 0.05
time_step = 0.01
drag_strength = 20.0
heating = 40.0
buoyancy = 10.0
helmholtz_shift = 0.001
local_shift = 0.5
coarse_shift = 0.02
gll_points = (
    -1.0,
    -0.8717401485096066,
    -0.5917001814331423,
    -0.2092992179024789,
    0.2092992179024789,
    0.5917001814331423,
    0.8717401485096066,
    1.0,
)
EZ = 16
NZ = 128
NV = 17


def legendre_seven(points):
    squared = points * points
    return points * (((429.0 * squared - 693.0) * squared + 315.0) * squared - 35.0) / 16.0


def jacobi_eigen(matrix):
    current = np.array(matrix)
    basis = np.eye(8)
    for _ in range(12):
        for first in range(7):
            for second in range(first + 1, 8):
                angle = 0.5 * math.atan2(
                    2.0 * float(current[first, second]),
                    float(current[second, second] - current[first, first]),
                )
                cosine = math.cos(angle)
                sine = math.sin(angle)
                rotation = np.eye(8)
                rotation[first, first] = cosine
                rotation[second, second] = cosine
                rotation[first, second] = sine
                rotation[second, first] = -sine
                current = rotation.T @ current @ rotation
                basis = basis @ rotation
    return (np.sum(current * np.eye(8), axis=0), basis)


def gll_tables():
    nodes = np.array(gll_points)
    values = legendre_seven(nodes)
    weights = 2.0 / (56.0 * values * values)
    differ = nodes[:, None] - nodes[None, :] + np.eye(8)
    derivative = values[:, None] / values[None, :] / differ * (1.0 - np.eye(8))
    ends = np.array([-14.0, 0.0, 0.0, 0.0, 0.0, 0.0, 0.0, 14.0])
    derivative = derivative + np.eye(8) * ends[None, :]
    stiffness = derivative.T @ (weights[:, None] * derivative)
    scaled = stiffness / np.sqrt(np.outer(weights, weights))
    scaled = 0.5 * (scaled + scaled.T)
    eigen_values, eigen_vectors = jacobi_eigen(scaled)
    eigen_basis = eigen_vectors / np.sqrt(weights)[:, None]
    return (nodes, weights, derivative, eigen_basis, np.maximum(eigen_values, 0.0))


def parts(table):
    table = np.asarray(table, np.float32)
    high = table.astype(ml_dtypes.bfloat16)
    low = (table - high.astype(np.float32)).astype(ml_dtypes.bfloat16)
    return high, low


def parts_three(table):
    high, low = parts(table)
    rest = np.asarray(table, np.float64) - high.astype(np.float64) - low.astype(np.float64)
    return high, low, rest.astype(ml_dtypes.bfloat16)


def left5(table):
    high, low, rest = parts_three(table)
    return np.concatenate([high, high, low, low, rest], axis=1)


def right5(table):
    return np.concatenate(parts_three(table), axis=0)


def left3(table):
    high, low = parts(table)
    return np.concatenate([high, high, low], axis=1)


def right3(table):
    return np.concatenate(parts(table), axis=0)


def split(field):
    high = field.astype(jnp.bfloat16)
    low = (field - high.astype(jnp.float32)).astype(jnp.bfloat16)
    return high, low


def stacked(field, terms, axis):
    high, low = split(field)
    order = [high, low, high, low, high] if terms == 5 else [high, low, high]
    return jnp.concatenate(order, axis=axis)


def lmul(table, field):
    terms = table.shape[1] // field.shape[0]
    return jnp.dot(table, stacked(field, terms, 0), preferred_element_type=jnp.float32)


def rmul(field, table):
    size = field.shape[1]
    part = [table[k : k + size] for k in range(0, table.shape[0], size)]
    order = [part[0], part[0], part[1], part[1], part[2]] if len(part) == 3 else [part[0]] + part
    return jnp.dot(
        stacked(field, len(order), 1),
        jnp.concatenate(order, axis=0),
        preferred_element_type=jnp.float32,
    )


def thrice(table, field):
    high, low = split(table)
    first, second = split(field)
    out = jnp.dot(high, first, preferred_element_type=jnp.float32)
    out = out + jnp.dot(high, second, preferred_element_type=jnp.float32)
    return out + jnp.dot(low, first, preferred_element_type=jnp.float32)


def lanes_of(field, size=64):
    return jnp.concatenate(
        [field[k * size : (k + 1) * size] for k in range(field.shape[0] // size)], axis=1
    )


def rows_of(field):
    return jnp.concatenate(
        [field[:, k * NZ : (k + 1) * NZ] for k in range(field.shape[1] // NZ)], axis=0
    )


def lane_index(rows):
    return lax.broadcasted_iota(jnp.int32, (rows, NZ), 1)


def turn(field, shift):
    if shift == 0:
        return field
    return pltpu.roll(field, shift % NZ, 1)


def join_z(field):
    lane = lane_index(field.shape[0])
    ahead = jnp.where((lane % 8 == 7) & (lane < NZ - 1), turn(field, -1), 0.0)
    behind = jnp.where((lane % 8 == 0) & (lane > 0), turn(field, 1), 0.0)
    return field + ahead + behind


def join_x(rows, count):
    blocks = [rows[k * 64 : (k + 1) * 64] for k in range(count)]
    sums = [blocks[k][0:8] + blocks[(k - 1) % count][56:64] for k in range(count)]
    pieces = []
    for k in range(count):
        pieces += [sums[k], blocks[k][8:56], sums[(k + 1) % count]]
    return jnp.concatenate(pieces, axis=0)


def fold(field):
    return jnp.sum(field.reshape(field.shape[0] // 8, 8, NZ), axis=0)


def total(field):
    return jnp.sum(jnp.sum(field, axis=0, keepdims=True), axis=1, keepdims=True)


def tiled(table, count):
    return jnp.concatenate([table] * count, axis=0)


class Tables:
    def __init__(self, nx, ny):
        nodes, w, d, e, lam = gll_tables()
        self.nx, self.ny = nx, ny
        eye8 = np.eye(8)
        kx = d.T @ (w[:, None] * d)
        bx = np.diag(w)
        eyez = np.eye(EZ)
        join = np.eye(NZ)
        for k in range(EZ - 1):
            join[8 * k + 7, 8 * k + 8] = 1.0
            join[8 * k + 8, 8 * k + 7] = 1.0
        dz_t = np.kron(eyez, d).T
        kz_t = np.kron(eyez, kx).T
        wz = np.tile(w, EZ)
        wxy = np.kron(w, w)
        mz = join.sum(axis=1)
        m1 = np.array([2.0, 1, 1, 1, 1, 1, 1, 2.0])
        mxy = np.kron(m1, m1)
        f32 = np.float32
        mass = np.outer(wxy, wz)
        self.mass = mass.astype(f32)
        self.wz = np.broadcast_to(wz[None, :], (64, NZ)).astype(f32)
        self.wxy = np.broadcast_to(wxy[:, None], (64, NZ)).astype(f32)
        self.inv_bm = (1.0 / (mass * np.outer(mxy, mz))).astype(f32)
        self.inv_m = (1.0 / np.outer(mxy, mz)).astype(f32)
        self.inv_mz = np.broadcast_to(1.0 / mz[None, :], (64, NZ)).astype(f32)
        self.visc = np.stack([self.mass, self.wz, self.wxy]).reshape(192, NZ)
        dx = np.kron(d, eye8)
        dy = np.kron(eye8, d)
        lv = np.kron(kx, bx) + np.kron(bx, kx)
        self.k1_left = left5(np.concatenate([dx, dy, lv], axis=0))
        self.k1_right = right5(np.concatenate([dz_t, kz_t], axis=1))
        self.div_left = left5(np.concatenate([dx, dy], axis=1))
        self.dz_right = right5(dz_t)
        hx = np.stack([(1.0 - nodes) / 2.0, (1.0 + nodes) / 2.0])
        self.hx = hx
        hz = np.zeros((NZ, NV))
        for z in range(NZ):
            hz[z, z // 8] = hx[0, z % 8]
            hz[z, z // 8 + 1] = hx[1, z % 8]
        pxy = np.zeros((8, 64))
        for xv in range(2):
            for yv in range(2):
                pxy[xv * 2 + yv] = np.kron(hx[xv], hx[yv])
        self.pxy_left = left3(pxy)
        hzm = np.zeros((NZ, NZ))
        hzm[:, :NV] = hz / mz[:, None]
        self.hzm_right = right3(hzm)
        self.hy = np.broadcast_to(hx.reshape(16, 1), (16, NZ)).astype(f32)

        def hartley(count):
            angle = 2.0 * np.pi / count * np.outer(np.arange(count), np.arange(count))
            return (np.cos(angle) + np.sin(angle)) / np.sqrt(count)

        self.hart_x = hartley(nx)
        hart_y = hartley(ny)
        ex = 2.0 - 2.0 * np.cos(2.0 * np.pi / nx * np.arange(nx))
        ey = 2.0 - 2.0 * np.cos(2.0 * np.pi / ny * np.arange(ny))
        ez = 2.0 - 2.0 * np.cos(np.pi / NV * np.arange(NV))
        levels = np.arange(NV)
        norms = np.where(levels == 0, np.sqrt(1.0 / NV), np.sqrt(2.0 / NV))
        cz = np.cos(np.pi / NV * np.outer(levels + 0.5, levels)) * norms[None, :]
        inverse = 1.0 / (
            2.0 * (ex[:, None, None] + ey[None, :, None] + ez[None, None, :]) + coarse_shift
        )
        shifted = np.roll(hart_y, -1, axis=1)
        self.hart_two = left3(np.concatenate([hart_y, shifted], axis=0))
        toward = np.zeros((24, nx * 8))
        for yv in range(2):
            for xv in range(2):
                for i in range(nx):
                    toward[yv * 12 : yv * 12 + nx, i * 8 + xv * 2 + yv] = self.hart_x[
                        :, (i + xv) % nx
                    ]
        self.toward_left = left3(toward)
        levels_only = np.zeros((NZ, NZ))
        levels_only[:NV, :NV] = cz
        self.levels_right = right3(levels_only)
        near = hart_y[(np.arange(ny + 8) - 1) % ny]
        self.near = near.astype(f32)
        czh = np.zeros((NZ, NZ))
        czh[:NV] = (hz @ cz).T
        self.czh_right = right3(czh)
        self.et_left = left3(np.kron(e.T, e.T))
        self.e_left = left3(np.kron(e, e))
        self.et_right = right3(np.kron(eyez, e))
        self.e_right = right3(np.kron(eyez, e.T) @ join)
        lxy = (lam[:, None] + lam[None, :]).reshape(64)
        self.scale = (1.0 / (lxy[:, None] + np.tile(lam, EZ)[None, :] + local_shift)).astype(f32)
        self.a_left = left5(lv + helmholtz_shift * np.kron(bx, bx))
        self.a_right = right5(np.concatenate([wz[:, None] * join, kz_t @ join], axis=0))
        back = np.zeros((24, nx * 8))
        for yv in range(2):
            for a in range(nx):
                for i in range(nx):
                    back[yv * 12 + a, i * 8 : i * 8 + 8] = self.hart_x[a, i] * hx[yv]
        self.back_left = left3(back)
        hzc = np.zeros((NZ, NZ))
        hzc[:, :NV] = (hz / mz[:, None]) @ cz
        self.hzc_right = right3(hzc)
        self.edge_left = left3(np.concatenate([np.kron(eye8, d[:1]), np.kron(eye8, d[7:])], axis=0))
        self.ex = ex
        ez_row = np.zeros((8, NZ))
        ez_row[:, :NV] = ez
        self.ez_row = ez_row.astype(f32)
        reach = np.zeros((nx, 4, nx))
        for i in range(nx):
            for xv in range(4):
                reach[i, xv] = self.hart_x[(i + xv - 1) % nx]
        self.reach = reach.reshape(-1).astype(f32)
        second = np.diag(2.0 * np.ones(NV)) - np.eye(NV, k=1) - np.eye(NV, k=-1)
        second[0, 0] = second[-1, -1] = 1.0
        double = 2.0 * np.ones(NV)
        double[0] = double[-1] = 1.0
        mass_z = np.diag(double) - second / 3.0
        both = np.zeros((NZ, 2 * NZ))
        both[:NV, :NV] = cz.T @ mass_z @ cz
        both[:NV, NZ : NZ + NV] = cz.T @ (second / 2.0) @ cz
        self.galerkin_right = right3(both)
        self.mx = 2.0 - ex / 3.0
        self.kx = ex / 2.0
        my = np.broadcast_to((2.0 - ey / 3.0)[:, None], (ny, NZ))
        ky = np.broadcast_to((ey / 2.0)[:, None], (ny, NZ))
        self.mky = np.concatenate([my, ky], axis=0).astype(f32)
        self.last_left = left5(np.concatenate([dx, dy], axis=0))
        self.d = d


def call(kernel, outs, *args, scratch=(), smem=0, space=pltpu.VMEM, limit=VMEM_LIMIT):
    specs = [pl.BlockSpec(memory_space=pltpu.SMEM)] * smem
    specs += [pl.BlockSpec(memory_space=space)] * (len(args) - smem)
    return pl.pallas_call(
        kernel,
        out_shape=[jax.ShapeDtypeStruct(shape, jnp.float32) for shape in outs],
        in_specs=specs,
        out_specs=[pl.BlockSpec(memory_space=pltpu.VMEM)] * len(outs),
        scratch_shapes=list(scratch),
        interpret=INTERPRET,
        compiler_params=pltpu.CompilerParams(vmem_limit_bytes=limit),
    )(*args)


def stage_rate(idx, h, *refs):
    sources, (fld, xa, xb, kp), landed, sems = refs[:5], refs[5:9], refs[9:14], refs[14]
    copies = [
        pltpu.make_async_copy(source, place, sems.at[k])
        for k, (source, place) in enumerate(zip(sources, landed))
    ]
    for copy in copies:
        copy.start()
    for copy in copies:
        copy.wait()
    flow, old, left, right, tab = landed
    f = [flow[q * 64 : q * 64 + 64] for q in range(4)]
    p = old[...]
    lx = lmul(left[...], jnp.concatenate(f + [p], axis=1))
    rx = rmul(jnp.concatenate(f + [p], axis=0), right[...])
    mass, wz, wxy = tab[0:64], tab[64:128], tab[128:192]
    u, v, w, theta = f
    drag = drag_strength * jnp.sqrt(u * u + v * v + w * w)
    canopy = (lane_index(64) // 8 < h[0, 0]).astype(jnp.float32)
    drag = drag * canopy
    forcing = [-drag * u, -drag * v, -drag * w + buoyancy * theta, heating * canopy]
    for q in range(5):
        lane = slice(q * NZ, q * NZ + NZ)
        rows = slice(q * 64, q * 64 + 64)
        gx, gy, lv = lx[0:64, lane], lx[64:128, lane], lx[128:192, lane]
        gz, kz = rx[rows, 0:NZ], rx[rows, NZ : 2 * NZ]
        stiff = lv * wz + wxy * kz
        if q < 4:
            rate = mass * (forcing[q] - (u * gx + v * gy + w * gz)) - viscosity * stiff
            fld[rows] = join_z(rate)
        else:
            kp[...] = stiff + helmholtz_shift * mass * p
            for k, grad in enumerate((gx, gy, gz)):
                fld[(4 + k) * 64 : (5 + k) * 64] = join_z(mass * grad)
    start = jnp.concatenate([fld[q * 64 : q * 64 + 8] for q in range(7)], axis=0)
    end = jnp.concatenate([fld[q * 64 + 56 : q * 64 + 64] for q in range(7)], axis=0)
    swap_out(is_odd(idx[0]), start, end, xa, xb)


def stage_faces(idx, fld, xa, xb, out, ya, yb):
    below, above = swap_in(is_odd(idx[0]), xa[...], xb[...])
    for q in range(7):
        base = q * 64
        out[base : base + 8] = fld[base : base + 8] + below[q * 8 : q * 8 + 8]
        out[base + 8 : base + 56] = fld[base + 8 : base + 56]
        out[base + 56 : base + 64] = fld[base + 56 : base + 64] + above[q * 8 : q * 8 + 8]
    swap_faces(is_odd(idx[1]), out, ya, yb)


def swap_faces(odd, ref, first, second):
    count = ref.shape[0] // 8
    start = ref[pl.ds(0, count, stride=8), :]
    end = ref[pl.ds(7, count, stride=8), :]
    swap_out(odd, start, end, first, second)


def put_faces(ref, below, above):
    count = ref.shape[0] // 8
    ref[pl.ds(0, count, stride=8), :] = ref[pl.ds(0, count, stride=8), :] + below
    ref[pl.ds(7, count, stride=8), :] = ref[pl.ds(7, count, stride=8), :] + above


def add_faces(odd, ref, first, second):
    put_faces(ref, *swap_in(odd, first[...], second[...]))


def swap_out(odd, start, end, first, second):
    first[...] = jnp.where(odd, start, end)
    second[...] = jnp.where(odd, end, start)


def swap_in(odd, first, second):
    return jnp.where(odd, first, second), jnp.where(odd, second, first)


def is_odd(index):
    return lax.rem(index, 2) == 1


def make_stages(t):
    nx, ny = t.nx, t.ny

    def stage_state(
        idx, fx, below, above, flow, kp, tab, dleft, dright, pleft, hright, prov, g0, piece, scr
    ):
        scr[...] = fx[...]
        add_faces(is_odd(idx[1]), scr, below, above)
        mass, inv_bm = tab[0:64], tab[64:128]
        lane = lane_index(64)
        new = []
        for q in range(4):
            rows = slice(q * 64, q * 64 + 64)
            value = flow[rows] + time_step * scr[rows] * inv_bm
            if q == 2:
                value = jnp.where((lane == 0) | (lane == NZ - 1), 0.0, value)
            prov[rows] = value
            new.append(value)
        for k in range(3):
            g0[k * 64 : k * 64 + 64] = scr[(4 + k) * 64 : (5 + k) * 64] * inv_bm
        div = lmul(dleft[...], jnp.concatenate(new[:2], axis=0)) + rmul(new[2], dright[...])
        joined = join_z(-mass * div - kp[...])
        piece[0:64] = joined
        piece[64:72] = rmul(lmul(pleft[...], joined), hright[...])


    def packed(modes, lane):
        return sum(turn(modes[8 * g : 8 * g + 8], lane + 20 * g) for g in range(3))

    def stage_ring(idx, ring, r, ra, rb):
        rows = jnp.concatenate([ring[i * 72 : i * 72 + 64] for i in range(nx)], axis=0)
        r[...] = join_x(rows, nx)
        swap_faces(is_odd(idx[1]), r, ra, rb)

    def stage_message(ring, toward, levels, msg):
        corners = jnp.concatenate([ring[i * 72 + 64 : i * 72 + 72] for i in range(nx)], axis=0)
        block = packed(rmul(lmul(toward[...], corners), levels[...]), 0)
        for k in range(ny):
            msg[k * 8 : k * 8 + 8] = block

    def smoothed(field, etl, etr, sc, er, el):
        modal = rmul(rows_of(lmul(etl, lanes_of(field))), etr)
        modal = rmul(modal * tiled(sc, nx), er)
        return rows_of(lmul(el, lanes_of(modal)))

    def stage_smooth(idx, r, ra, rb, etl, etr, sc, er, el, r0, s, s0, s7):
        r0[...] = r[...]
        add_faces(is_odd(idx[1]), r0, ra, rb)
        local = smoothed(r0[...], etl[...], etr[...], sc[...], er[...], el[...])
        s[...] = join_x(local, nx)
        swap_faces(is_odd(idx[1]), s, s0, s7)

    def spectra(rec, stride, hart):
        cells = jnp.concatenate([rec[pl.ds(k, ny, stride=stride), :] for k in range(8)], axis=1)
        both = lmul(hart, cells)

        def mode(a, lane):
            tile, shift = slice((a % 8) * NZ, (a % 8 + 1) * NZ), -lane - 20 * (a // 8)
            line = turn(both[0:ny, tile], shift)
            n = 12 + a
            tile, shift = slice((n % 8) * NZ, (n % 8 + 1) * NZ), -lane - 20 * (n // 8)
            return line + turn(both[ny : 2 * ny, tile], shift)

        return mode

    def solved(comb, a, ez_row, ky):
        levels = 2.0 * (2.0 * ky + ez_row) + coarse_shift
        return jnp.where(
            lane_index(ny) < NV, comb / (levels + 2.0 * float(t.ex[a])), 0.0
        )

    def stage_coarse(idx, rec, hart, ez_row, mky, around, czh, out):
        mode = spectra(rec, 8, hart[...])
        ky = mky[ny : 2 * ny]
        wide = jnp.concatenate(
            [solved(mode(a, 0), a, ez_row[0:1], ky) for a in range(nx)], axis=1
        )
        lines = thrice(around[pl.ds(idx[1], 8), :], wide)
        columns = []
        for i in range(nx):
            acc = lines[:, 0:NZ] * float(t.hart_x[i, 0])
            for a in range(1, nx):
                acc = acc + lines[:, a * NZ : (a + 1) * NZ] * float(t.hart_x[i, a])
            columns.append(acc)
        out[...] = rmul(jnp.concatenate(columns, axis=0), czh[...])

    def applied(field, al, wxy, ar):
        side = rows_of(lmul(al, lanes_of(field)))
        return rmul(jnp.concatenate([side, field * tiled(wxy, nx)], axis=1), ar)

    def restricted(field, back, hzc):
        columns = []
        for i in range(nx):
            acc = None
            for x in range(8):
                here = field[i * 64 + x * 8 : i * 64 + x * 8 + 8] * float(t.hx[0, x])
                k = (i - 1) % nx
                there = field[k * 64 + x * 8 : k * 64 + x * 8 + 8] * float(t.hx[1, x])
                acc = here + there if acc is None else acc + here + there
            columns.append(acc)
        return rmul(lmul(back, jnp.concatenate(columns, axis=0)), hzc)

    def stage_apply(
        idx, s, below, above, vert, r0, hy, al, tab, ar, back, hzc, z0, q, q0, q7, cq, sums
    ):
        z0[...] = s[...]
        add_faces(is_odd(idx[1]), z0, below, above)
        slabs = []
        for i in range(nx):
            slabs.append(
                hy[0:8] * vert[i * 8 + 1 : i * 8 + 2] + hy[8:16] * vert[i * 8 + 2 : i * 8 + 3]
            )
        pieces = []
        for i in range(nx):
            for x in range(8):
                pieces.append(
                    slabs[i] * float(t.hx[0, x]) + slabs[(i + 1) % nx] * float(t.hx[1, x])
                )
        field = z0[...] + jnp.concatenate(pieces, axis=0)
        z0[...] = field
        wxy, inv_m, inv_mz = tab[0:64], tab[64:128], tab[128:192]
        image = applied(field, al[...], wxy, ar[...])
        sums[0:8] = fold(r0[...] * field * tiled(inv_m, nx))
        sums[8:16] = fold(field * image * tiled(inv_mz, nx))
        cq[...] = restricted(image, back[...], hzc[...])
        q[...] = join_x(image, nx)
        swap_faces(is_odd(idx[1]), q, q0, q7)

    def stage_again(
        idx, q, below, above, z0, edge, tab, etl, etr, sc, er, el, s, s0, s7, sums, scr
    ):
        scr[...] = q[...]
        add_faces(is_odd(idx[1]), scr, below, above)
        field = scr[...]
        local = smoothed(field, etl[...], etr[...], sc[...], er[...], el[...])
        sums[...] = fold(field * local * tiled(tab[...], nx))
        s[...] = join_x(local, nx)
        size = nx * 8
        odd = is_odd(idx[1])
        swap_out(
            odd,
            s[pl.ds(0, size, stride=8), :],
            s[pl.ds(7, size, stride=8), :],
            s0.at[0:size],
            s7.at[0:size],
        )
        base = pl.multiple_of(idx[0] * 64, 64)
        start, end = slopes(z0[pl.ds(base, 64), :], edge[...])
        swap_out(odd, start, end, s0.at[size : size + 8], s7.at[size : size + 8])

    def slopes(field, edge):
        both = lmul(edge, field)
        return both[0:8], both[8:16]

    def stage_gather(
        idx, s, first, second, z0, cq, sums1, sums2, al, tab, ar, back, hzc, edge, sq, msg, ends
    ):
        odd = is_odd(idx[1])
        size = nx * 8
        faces = swap_in(odd, first[0:size], second[0:size])
        below, above = swap_in(odd, first[size : size + 8], second[size : size + 8])
        ends[0:8] = below
        ends[8:16] = above
        sq[...] = s[...]
        put_faces(sq, *faces)
        field = sq[...]
        wxy, inv_mz = tab[0:64], tab[128:192]
        image = applied(field, al[...], wxy, ar[...])
        last = total(fold(field * image * tiled(inv_mz, nx)))
        tq = restricted(image, back[...], hzc[...])
        block = packed(cq[...], 0) + packed(tq, 60)
        lane = lane_index(8)
        row = lax.broadcasted_iota(jnp.int32, (8, NZ), 0)
        values = [total(sums1[0:8]), total(sums1[8:16]), total(sums2[...]), last]
        for k, value in enumerate(values):
            block = block + jnp.where((row == 0) & (lane == 120 + k), value, 0.0)
        base = pl.multiple_of(idx[0] * 64, 64)
        start, end = slopes(sq[pl.ds(base, 64), :], edge[...])
        for k in range(ny):
            msg[k * 16 : k * 16 + 8] = block
            msg[k * 16 + 8 : k * 16 + 16] = start
        after = lax.rem(idx[1] + 1, ny)
        msg[pl.ds(pl.multiple_of(after * 16 + 8, 8), 8), :] = end

    def stage_final(
        idx,
        reach,
        rec,
        ends,
        z0,
        sq,
        prov,
        g0,
        old,
        hart,
        ez_row,
        around,
        czh,
        gal,
        mky,
        hy,
        left,
        right,
        inv_mz,
        new,
        press,
        scr,
    ):
        my, ky = mky[0:ny], mky[ny : 2 * ny]
        cross = jnp.zeros((ny, NZ), jnp.float32)
        plain = jnp.zeros((ny, NZ), jnp.float32)
        found = []
        mode = spectra(rec, 16, hart[...])
        for a in range(nx):
            comb = mode(a, 0)
            e = solved(comb, a, ez_row[0:1], ky)
            found.append(e)
            plain = plain + e * comb
            cross = cross + e * mode(a, 60)
        grown = rmul(jnp.concatenate(found, axis=0), gal[...])
        quad = jnp.zeros((ny, NZ), jnp.float32)
        for a in range(nx):
            rows = slice(a * ny, (a + 1) * ny)
            mxa, kxa = float(t.mx[a]), float(t.kx[a])
            weight_m = my * (kxa + helmholtz_shift * mxa) + ky * mxa
            weight_k = my * mxa
            quad = quad + found[a] * (
                weight_m * grown[rows, 0:NZ] + weight_k * grown[rows, NZ : 2 * NZ]
            )
        scalars = jnp.sum(rec[pl.ds(0, ny, stride=16), :], axis=0, keepdims=True)
        line = lane_index(1)

        def pick(k):
            return jnp.sum(jnp.where(line == 120 + k, scalars, 0.0), axis=1, keepdims=True)

        rz0, zq0 = pick(0), pick(1)
        wq = pick(2) + total(plain)
        ww = pick(3) + 2.0 * total(cross) + total(quad)
        first = rz0 / zq0
        rz1 = rz0 - 2.0 * first * zq0 + first * first * wq
        beta = rz1 / rz0
        grow = 1.0 + beta
        curve = grow * grow * zq0 - 2.0 * grow * first * wq + first * first * ww
        second = rz1 / curve
        on_z = first + second * grow
        on_w = -second * first
        lines = thrice(around[pl.ds(idx[1], 8), :], jnp.concatenate(found, axis=1))
        stack = []
        for xv in range(4):
            base = (idx[0] * 4 + xv) * nx
            acc = lines[:, 0:NZ] * reach[base]
            for a in range(1, nx):
                acc = acc + lines[:, a * NZ : (a + 1) * NZ] * reach[base + a]
            stack.append(acc)
        scr[...] = rmul(jnp.concatenate(stack, axis=0), czh[...]) * on_w
        hy0, hy1 = hy[0:8], hy[8:16]
        slabs = [hy0 * scr[k * 8 + 1 : k * 8 + 2] + hy1 * scr[k * 8 + 2 : k * 8 + 3] for k in range(4)]
        coarse = jnp.concatenate(
            [slabs[1] * float(t.hx[0, x]) + slabs[2] * float(t.hx[1, x]) for x in range(8)], axis=0
        )

        def own(shift):
            base = pl.multiple_of(lax.rem(idx[0] + shift + nx, nx) * 64, 64)
            return z0[pl.ds(base, 64), :] * on_z + sq[pl.ds(base, 64), :] * on_w

        change = own(0) + coarse
        press[...] = old[...] + change
        slopes = lmul(left[...], change)
        gx, gy = slopes[0:64], slopes[64:128]
        gz = rmul(change, right[...])
        prior, later = own(-1), own(1)
        edge0 = 0.5 * (slabs[1] - slabs[0])
        edge7 = 0.5 * (slabs[3] - slabs[2])
        for x in range(8):
            edge0 = edge0 + prior[x * 8 : x * 8 + 8] * float(t.d[7, x])
            edge7 = edge7 + later[x * 8 : x * 8 + 8] * float(t.d[0, x])
        new[0:8] = prov[0:8] - g0[0:8] - 0.5 * (gx[0:8] + edge0)
        new[8:56] = prov[8:56] - g0[8:56] - gx[8:56]
        new[56:64] = prov[56:64] - g0[56:64] - 0.5 * (gx[56:64] + edge7)
        hx0, hx1 = hy0, hy1
        step0 = [0.5 * (scr[k * 8 + 1 : k * 8 + 2] - scr[k * 8 : k * 8 + 1]) for k in (1, 2)]
        step7 = [0.5 * (scr[k * 8 + 3 : k * 8 + 4] - scr[k * 8 + 2 : k * 8 + 3]) for k in (1, 2)]
        before = lax.rem(idx[1] + ny - 1, ny)
        after = lax.rem(idx[1] + 1, ny)
        below = rec[pl.ds(pl.multiple_of(before * 16 + 8, 8), 8), :]
        above = rec[pl.ds(pl.multiple_of(after * 16 + 8, 8), 8), :]
        under = ends[0:8] * on_z + below * on_w + hx0 * step0[0] + hx1 * step0[1]
        over = ends[8:16] * on_z + above * on_w + hx0 * step7[0] + hx1 * step7[1]
        press_y = gy
        new[64:128] = press_y
        own0 = new[pl.ds(64, 8, stride=8), :]
        own7 = new[pl.ds(71, 8, stride=8), :]
        new[pl.ds(64, 8, stride=8), :] = 0.5 * (own0 + under)
        new[pl.ds(71, 8, stride=8), :] = 0.5 * (own7 + over)
        new[64:128] = prov[64:128] - g0[64:128] - new[64:128]
        new[128:192] = prov[128:192] - g0[128:192] - join_z(gz) * inv_mz[...]
        new[192:256] = prov[192:256]

    return (
        stage_state,
        stage_ring,
        stage_message,
        stage_smooth,
        stage_coarse,
        stage_apply,
        stage_again,
        stage_gather,
        stage_final,
    )


def exchange(axis, first, second):
    count = lax.axis_size(axis)
    pairs = [(k, k ^ 1) for k in range(count)]
    across = [(k, ((k - 1) ^ 1) + 1) for k in range(1, count - 1)] + [(0, count - 1), (count - 1, 0)]
    return lax.ppermute(first, axis, pairs), lax.ppermute(second, axis, across)


def make_device(t):
    nx, ny = t.nx, t.ny
    (
        stage_state,
        stage_ring,
        stage_message,
        stage_smooth,
        stage_coarse,
        stage_apply,
        stage_again,
        stage_gather,
        stage_final,
    ) = make_stages(t)
    c = jnp.asarray
    col, ring, face, more = (64, NZ), (nx * 64, NZ), (nx * 8, NZ), (nx * 8 + 8, NZ)

    def on_device(flow_state, building_height, pressure_old):
        flow = flow_state.reshape(256, NZ)
        old = pressure_old.reshape(64, NZ)
        idx = jnp.stack([lax.axis_index("gx"), lax.axis_index("gy")]).astype(jnp.int32)
        fld, xf0, xf7, kp = call(
            stage_rate,
            [(448, NZ), (56, NZ), (56, NZ), col],
            idx,
            building_height,
            flow,
            old,
            c(t.k1_left),
            c(t.k1_right),
            c(t.visc),
            smem=2,
            space=pltpu.HBM,
            limit=60 * 1024 * 1024,
            scratch=[
                pltpu.VMEM((256, NZ), jnp.float32),
                pltpu.VMEM((64, NZ), jnp.float32),
                pltpu.VMEM(t.k1_left.shape, jnp.bfloat16),
                pltpu.VMEM(t.k1_right.shape, jnp.bfloat16),
                pltpu.VMEM(t.visc.shape, jnp.float32),
                pltpu.SemaphoreType.DMA((5,)),
            ],
        )
        below, above = exchange("gx", xf0, xf7)
        fld, yf0, yf7 = call(
            stage_faces, [(448, NZ), (56, NZ), (56, NZ)], idx, fld, below, above, smem=1
        )
        below, above = exchange("gy", yf0, yf7)
        prov, g0, piece = call(
            stage_state,
            [(256, NZ), (192, NZ), (72, NZ)],
            idx,
            fld,
            below,
            above,
            flow,
            kp,
            c(np.concatenate([t.mass, t.inv_bm])),
            c(t.div_left),
            c(t.dz_right),
            c(t.pxy_left),
            c(t.hzm_right),
            smem=1,
            scratch=[pltpu.VMEM((448, NZ), jnp.float32)],
        )
        whole = lax.all_gather(piece, "gx", axis=0, tiled=True)
        r, ra, rb = call(stage_ring, [ring, face, face], idx, whole, smem=1)
        below, above = exchange("gy", ra, rb)
        (msg,) = call(
            stage_message, [(ny * 8, NZ)], whole, c(t.toward_left), c(t.levels_right)
        )
        rec = lax.all_to_all(msg.reshape(ny, 8, NZ), "gy", 0, 0, tiled=True)
        smoother = (c(t.et_left), c(t.et_right), c(t.scale), c(t.e_right), c(t.e_left))
        r0, s, s0, s7 = call(
            stage_smooth, [ring, ring, face, face], idx, r, below, above, *smoother, smem=1
        )
        below, above = exchange("gy", s0, s7)
        (vert,) = call(
            stage_coarse,
            [face],
            idx,
            rec.reshape(ny * 8, NZ),
            c(t.hart_two),
            c(t.ez_row),
            c(t.mky),
            c(t.near),
            c(t.czh_right),
            smem=1,
        )
        tab = c(np.concatenate([t.wxy, t.inv_m, t.inv_mz]))
        operator = (c(t.a_left), tab, c(t.a_right), c(t.back_left), c(t.hzc_right))
        z0, q, q0, q7, cq, sums1 = call(
            stage_apply,
            [ring, ring, face, face, (24, NZ), (16, NZ)],
            idx,
            s,
            below,
            above,
            vert,
            r0,
            c(t.hy),
            *operator,
            smem=1,
        )
        below, above = exchange("gy", q0, q7)
        s, s0, s7, sums2 = call(
            stage_again,
            [ring, more, more, (8, NZ)],
            idx,
            q,
            below,
            above,
            z0,
            c(t.edge_left),
            c(t.inv_mz),
            *smoother,
            smem=1,
            scratch=[pltpu.VMEM(ring, jnp.float32)],
        )
        below, above = exchange("gy", s0, s7)
        sq, msg, ends = call(
            stage_gather,
            [ring, (ny * 16, NZ), (16, NZ)],
            idx,
            s,
            below,
            above,
            z0,
            cq,
            sums1,
            sums2,
            *operator,
            c(t.edge_left),
            smem=1,
        )
        rec = lax.all_to_all(msg.reshape(ny, 16, NZ), "gy", 0, 0, tiled=True)
        new, press = call(
            stage_final,
            [(256, NZ), col],
            idx,
            c(t.reach),
            rec.reshape(ny * 16, NZ),
            ends,
            z0,
            sq,
            prov,
            g0,
            old,
            c(t.hart_two),
            c(t.ez_row),
            c(t.near),
            c(t.czh_right),
            c(t.galerkin_right),
            c(t.mky),
            c(t.hy),
            c(t.last_left),
            c(t.dz_right),
            c(t.inv_mz),
            smem=2,
            scratch=[pltpu.VMEM((32, NZ), jnp.float32)],
        )
        return new.reshape(flow_state.shape), press.reshape(pressure_old.shape)

    return on_device


def solution(mesh):
    t = Tables(mesh.shape["gx"], mesh.shape["gy"])
    in_specs = (P(None, "gx", "gy", None), P("gx", "gy"), P("gx", "gy", None))
    out_specs = (P(None, "gx", "gy", None), P("gx", "gy", None))
    return jax.shard_map(
        make_device(t), mesh=mesh, in_specs=in_specs, out_specs=out_specs, check_vma=False
    )
```
